1024 devices in a mesh: gx: 16 (over z), gy: 16 (over y, core), gz: 4 (over x).
Axes of the slice: x: 4, y: 8, z: 16, core: 2. Of those that a mesh axis runs over, the one named last changes fastest.
Arguments:
- positions: float32 [3, 32, 32, 8, 128], P(None, 'gx', 'gy', 'gz'), may hold values from 0 to 12
- charges: float32 [32, 32, 8, 128], P('gx', 'gy', 'gz'), may hold values from -3 to 3
- atom_types: int32 [32, 32, 8, 128], P('gx', 'gy', 'gz'), may hold values from 0 to 127
- atom_counts: int32 [32, 32, 8], P('gx', 'gy', 'gz'), may hold values from 48 to 128, as said below
- type_sigma: float32 [128], replicated, may hold values from 1 to 3.2
- type_epsilon: float32 [128], replicated, may hold values from 0.02 to 0.5
- pair_list: int32 [2, 16, 16, 4, 188], P(None, 'gx', 'gy', 'gz'), may hold values from -1 to 26, as said below
Outputs:
- forces: float32 [3, 32, 32, 8, 128], P(None, 'gx', 'gy', 'gz')
The draws below stay inside these ranges and needn't reach their ends.
Inputs may be any that keep to these rules, and one draw needn't show every extreme that they name: The first atom_counts[c] slots of cell c hold atoms; some cell holds 128. `pair_list`: row 0 holds a local cell index below 8, row 1 a neighbour code of 0 to 26 or -1 for an empty slot; empty slots come after the listed ones. Over all blocks each cell is listed with itself (code 13) exactly once, and each unordered pair of distinct neighbouring cells at most once; pairs that the list leaves out are not computed. Some block lists exactly 188 pairs.
All inputs are finite; a program needn't handle non-finite values.
Results may differ from the reference program's by a relative error of at most 0.0003.
Values sent between devices are 32-bit elements; how exact they have to be, the bound alone decides.
No kernel may reach another device: no remote copies, remote signals or barrier semaphores. Data moves between devices by JAX's collectives and lax.ppermute only.
A program may use at most 32 MiB of HBM per device.

```python
import math
import jax
import jax.numpy as jnp
import numpy as np
from jax import lax

CX = 2
CY = 2
CZ = 2
CAP = 128
NTYPES = 128
NX = 32
NY = 32
NZ = 8
PAIRS = 188
N_GX = 16
N_GY = 16
N_GZ = 4


def draw_atom_counts(key, part):
    key_fill = jax.random.fold_in(key, 11)
    key_pick = jax.random.fold_in(key, 12)
    counts = jax.random.randint(key_fill, (NX * NY * NZ,), CAP * 3 // 8, CAP + 1, dtype=jnp.int32)
    chosen = jax.random.randint(key_pick, (), 0, NX * NY * NZ, dtype=jnp.int32)
    counts = counts.at[chosen].set(CAP)
    return counts.reshape(NX, NY, NZ).astype(jnp.int32)


def draw_pair_list(key, part):
    blocks_first = NX // CX
    blocks_second = NY // CY
    blocks_third = NZ // CZ
    cells_block = CX * CY * CZ
    owner_bits = jax.random.randint(jax.random.fold_in(key, 21), (NX, NY, NZ, 13), 0, 2, dtype=jnp.int32)
    keep_draw = jax.random.randint(jax.random.fold_in(key, 22), (NX, NY, NZ, 13), 0, 4, dtype=jnp.int32)
    chosen = jax.random.randint(jax.random.fold_in(key, 23), (), 0, blocks_first * blocks_second * blocks_third, dtype=jnp.int32)
    along_first = jnp.arange(NX, dtype=jnp.int32) // CX
    along_second = jnp.arange(NY, dtype=jnp.int32) // CY
    along_third = jnp.arange(NZ, dtype=jnp.int32) // CZ
    block_of_cell = (along_first[:, None, None] * blocks_second + along_second[None, :, None]) * blocks_third + along_third[None, None, :]
    forced = (block_of_cell == chosen).astype(jnp.int32)
    columns = [None] * 27
    columns[13] = jnp.ones((NX, NY, NZ), jnp.int32)
    for forward in range(13):
        code_value = 14 + forward
        offset = (code_value // 9 - 1, code_value // 3 % 3 - 1, code_value % 3 - 1)
        forced_far = jnp.roll(forced, (-offset[0], -offset[1], -offset[2]), (0, 1, 2))
        lower_owns = jnp.where(forced == 1, 1, jnp.where(forced_far == 1, 0, owner_bits[..., forward]))
        kept = jnp.where((forced == 1) | (forced_far == 1), 1, (keep_draw[..., forward] != 0).astype(jnp.int32))
        columns[code_value] = lower_owns * kept
        columns[12 - forward] = jnp.roll((1 - lower_owns) * kept, offset, (0, 1, 2))
    listed = jnp.stack(columns, -1)
    listed = listed.reshape(blocks_first, CX, blocks_second, CY, blocks_third, CZ, 27).transpose(0, 2, 4, 1, 3, 5, 6)
    listed = listed.reshape(blocks_first, blocks_second, blocks_third, cells_block * 27)
    candidate = jnp.arange(cells_block * 27, dtype=jnp.int32)
    sort_key = (1 - listed) * (cells_block * 27) + candidate
    chosen_order = jnp.argsort(sort_key, axis=-1)[..., :PAIRS]
    listed_sorted = jnp.take_along_axis(listed, chosen_order, -1)
    cell_ids = chosen_order // 27
    code_ids = jnp.where(listed_sorted == 1, chosen_order % 27, -1)
    return jnp.stack([cell_ids, code_ids]).astype(jnp.int32)


def plant(result, own_key, least, top_value):
    shape = result.shape
    spot = [jax.random.randint(jax.random.fold_in(own_key, axis), (), 0, shape[axis]) for axis in range(len(shape))]
    result = result.at[tuple(spot)].set(least)
    longest = shape.index(max(shape))
    spot[longest] = (spot[longest] + 1) % shape[longest]
    return result.at[tuple(spot)].set(top_value)


def steps_of(rng, dims, pieces, low, high):
    level = 1.0
    for position, blocks in pieces:
        steps = jax.random.uniform(jax.random.fold_in(jax.random.fold_in(rng, 6), position), (blocks,), jnp.float32, low / len(pieces), high / len(pieces))
        level = level * jnp.repeat(jnp.exp(steps), dims[position] // blocks).reshape((-1,) + (1,) * (len(dims) - 1 - position))
    return level


def rank_bounds(amount, skew):
    portions = [(1 << 20) // math.isqrt(grade ** skew) + 1 for grade in range(1, amount + 1)]
    spread = 1 + sum(portions) // (1 << 30)
    return np.cumsum(np.array([max(1, weight // spread) for weight in portions]))


def ranked(own_key, shape, count, slope):
    grid = rank_bounds(count, slope)
    ticket = jax.random.randint(jax.random.fold_in(own_key, 1), shape, 0, int(grid[count - 1]))
    rank = jnp.searchsorted(jnp.asarray(grid, jnp.int32), ticket, side="right")
    return jax.random.permutation(jax.random.fold_in(own_key, 2), count)[rank].astype(jnp.int32)


def noise(own_key, dims, scale, reach, split=(), kind=jnp.bfloat16):
    values = jax.random.normal(own_key, dims, jnp.float32) * scale
    if len(split) > 0:
        values = steps_of(own_key, dims, split, -0.22, 0.18) * values
    return jnp.clip(values, min=-reach, max=reach).astype(kind)


def setup_inputs(seed: int = 0) -> dict:
    key_of = jax.random.split(jax.random.key(seed), 8)
    positions = jnp.clip(12.0 * jax.random.uniform(key_of[0], (3, NX, NY, NZ, CAP), jnp.float32) ** steps_of(key_of[0], (3, NX, NY, NZ, CAP), ((1, 16), (2, 16), (3, 4)), -0.2, 0.2), 0.0, 12.0)
    charges = noise(key_of[1], (NX, NY, NZ, CAP), 0.5, 3.0, ((0, 16), (1, 16), (2, 4)), jnp.float32)
    atom_types = plant(ranked(key_of[2], (NX, NY, NZ, CAP), NTYPES, 2), jax.random.fold_in(key_of[2], 3), 0, NTYPES - 1).astype(jnp.int32)
    atom_counts = draw_atom_counts(jax.random.fold_in(key_of[7], 71), 0)
    type_sigma = jnp.clip(jnp.exp(jax.random.uniform(key_of[4], (NTYPES,), jnp.float32, math.log(1.0), math.log(3.2))), 1.0, 3.2)
    type_epsilon = jnp.clip(jnp.exp(jax.random.uniform(key_of[5], (NTYPES,), jnp.float32, math.log(0.02), math.log(0.5))), 0.02, 0.5)
    pair_list = draw_pair_list(jax.random.fold_in(key_of[7], 71), 0)
    return dict(positions=positions, charges=charges, atom_types=atom_types, atom_counts=atom_counts, type_sigma=type_sigma, type_epsilon=type_epsilon, pair_list=pair_list)


cell_edge = 12.0
switch_on = 100.0
cutoff_sq = 144.0
switch_den = 44.0 * 44.0 * 44.0
block_pairs = 12

def table_lookup(type_codes, live_slots, type_sigma, root_depth):
    catalog = jnp.arange(type_sigma.shape[0]).astype(type_codes.dtype)
    matches = type_codes[..., None] == catalog
    sigma_atom = jnp.where(live_slots, lax.optimization_barrier(jnp.sum(jnp.where(matches, type_sigma, 0.0), -1)), 1.0)
    depth_atom = jnp.where(live_slots, lax.optimization_barrier(jnp.sum(jnp.where(matches, root_depth, 0.0), -1)), 0.0)
    return (sigma_atom, depth_atom)

def decode(code_ids):
    valid_slot = code_ids >= 0
    safe_code = jnp.where(valid_slot, code_ids, 13)
    move_first = safe_code // 9 - 1
    move_second = safe_code // 3 % 3 - 1
    move_third = safe_code % 3 - 1
    weight = jnp.where(valid_slot, jnp.where(safe_code == 13, 0.5, 1.0), 0.0)
    return (move_first, move_second, move_third, weight)

def pair_forces(left_atoms, right_atoms, offset):
    separation = [left_atoms[component][:, :, None] - right_atoms[component][:, None, :] + offset[component][:, None, None] for component in range(3)]
    dist_sq = separation[0] * separation[0] + separation[1] * separation[1] + separation[2] * separation[2]
    sigma_mean = 0.5 * (left_atoms[4][:, :, None] + right_atoms[4][:, None, :])
    sigma_sq = sigma_mean * sigma_mean
    soft_sq = dist_sq + sigma_sq
    inverse = 1.0 / soft_sq
    size_ratio = sigma_sq * inverse
    third_power = size_ratio * size_ratio * size_ratio
    well_depth = 4.0 * left_atoms[5][:, :, None] * right_atoms[5][:, None, :]
    coulomb = left_atoms[3][:, :, None] * right_atoms[3][:, None, :] * lax.rsqrt(soft_sq)
    energy = well_depth * (third_power * third_power - third_power) + coulomb
    energy_slope = (well_depth * (3.0 * third_power - 6.0 * third_power * third_power) - 0.5 * coulomb) * inverse
    clipped = jnp.clip(dist_sq, switch_on, cutoff_sq)
    switch = (cutoff_sq - clipped) * (cutoff_sq - clipped) * (cutoff_sq + 2.0 * clipped - 3.0 * switch_on) / switch_den
    switch_slope = 6.0 * (cutoff_sq - clipped) * (switch_on - clipped) / switch_den
    pair_scale = -2.0 * (switch_slope * energy + switch * energy_slope)
    on_left = jnp.stack([lax.optimization_barrier(jnp.sum(pair_scale * component, 2)) for component in separation])
    on_right = -jnp.stack([lax.optimization_barrier(jnp.sum(pair_scale * component, 1)) for component in separation])
    return (on_left, on_right)

def reference(positions, charges, atom_types, atom_counts, type_sigma, type_epsilon, pair_list):
    live_slots = lax.broadcasted_iota(jnp.int32, charges.shape, 3) < atom_counts[..., None]
    charge_atom = jnp.where(live_slots, charges, 0.0)
    root_depth = jnp.sqrt(type_epsilon)
    sigma_atom, depth_atom = table_lookup(atom_types, live_slots, type_sigma, root_depth)
    atoms = jnp.concatenate([positions, jnp.stack([charge_atom, sigma_atom, depth_atom])], 0)
    total_cells = NX * NY * NZ
    flat_atoms = atoms.reshape(6, total_cells, CAP)
    block_total = N_GX * N_GY * N_GZ
    padded = (PAIRS + block_pairs - 1) // block_pairs * block_pairs
    cell_lists = jnp.pad(pair_list[0].reshape(block_total, PAIRS), ((0, 0), (0, padded - PAIRS)))
    code_lists = jnp.pad(pair_list[1].reshape(block_total, PAIRS), ((0, 0), (0, padded - PAIRS)), constant_values=-1)

    def device_step(forces, inputs):
        device, cell_all, code_all = inputs
        block_first = device // (N_GY * N_GZ)
        block_second = device // N_GZ % N_GY
        block_third = device % N_GZ
        live_pairs = jnp.sum((code_all >= 0).astype(jnp.int32)).astype(jnp.int32)
        block_count = (live_pairs + block_pairs - 1) // block_pairs

        def block_step(block_index, forces):
            first_slot = block_index * block_pairs
            cell_ids = lax.dynamic_slice_in_dim(cell_all, first_slot, block_pairs)
            code_ids = lax.dynamic_slice_in_dim(code_all, first_slot, block_pairs)
            move_first, move_second, move_third, weight = decode(code_ids)
            global_first = block_first * CX + cell_ids // (CY * CZ)
            global_second = block_second * CY + cell_ids // CZ % CY
            global_third = block_third * CZ + cell_ids % CZ
            home_cell = (global_first * NY + global_second) * NZ + global_third
            other_cell = ((global_first + move_first) % NX * NY + (global_second + move_second) % NY) * NZ + (global_third + move_third) % NZ
            left_atoms = jnp.take(flat_atoms, home_cell, axis=1)
            right_atoms = jnp.take(flat_atoms, other_cell, axis=1)
            offset = -cell_edge * jnp.stack([move_first, move_second, move_third]).astype(flat_atoms.dtype)
            on_left, on_right = pair_forces(left_atoms, right_atoms, offset)
            forces = forces.at[:, home_cell].add(on_left * weight[None, :, None])
            return forces.at[:, other_cell].add(on_right * weight[None, :, None])
        return (lax.fori_loop(0, block_count, block_step, forces), None)
    devices = jnp.arange(block_total, dtype=jnp.int32)
    start_forces = jnp.zeros((3, total_cells, CAP), flat_atoms.dtype)
    forces, unused = lax.scan(device_step, start_forces, (devices, cell_lists, code_lists))
    return forces.reshape(3, NX, NY, NZ, CAP)
```

```python
import math

import jax
import jax.numpy as jnp
from jax import lax
from jax.experimental import pallas as pl
from jax.experimental.pallas import tpu as pltpu
from jax.sharding import PartitionSpec as P

AXES = ("gx", "gy", "gz")
CUT = 144.0
WIDTH = 44.0
UNIT = 1.0 / math.sqrt(WIDTH)
EDGE = 12.0 * UNIT
CHARGE_UNIT = WIDTH ** -0.25
DEPTH_UNIT = math.sqrt(24.0)
FORCE_UNIT = 2.0 / WIDTH * math.sqrt(WIDTH)
COUNT_LANE = 27
META_ROW = 6
RELATIONS = [(r // 4, r // 2 % 2, r % 2) for r in range(1, 8)]
MAX_CHUNKS = 30


def parities():
    return [lax.rem(lax.axis_index(name), 2) for name in AXES]


def free_cells(relation, fixed, choices):
    spans = [[fixed[a]] if relation[a] else list(range(choices)) for a in range(3)]
    return [(x, y, z) for x in spans[0] for y in spans[1] for z in spans[2]]


def atoms_kernel(pos_ref, charge_ref, type_ref, count_ref, sigma_ref, eps_ref, pair_ref, own_ref, send_ref, rows_ref, kinds_ref, codes_ref):
    for i in range(2):
        for j in range(2):
            at = pl.ds(4 * i + 2 * j, 2)
            for comp in range(3):
                rows_ref[comp, at, :] = pos_ref[comp, i, j]
            rows_ref[3, at, :] = charge_ref[i, j]
            kinds_ref[at, :] = type_ref[i, j]
    codes_ref[...] = jnp.full(codes_ref.shape, -1, jnp.int32)
    slots = pair_ref.shape[-1]
    codes_ref[0:1, 0:slots] = pair_ref[0, 0, 0]
    codes_ref[1:2, 0:slots] = pair_ref[1, 0, 0]

    cell = lax.broadcasted_iota(jnp.int32, (8, 128), 0)
    lane = lax.broadcasted_iota(jnp.int32, (8, 128), 1)
    count = jnp.zeros((8, 128), jnp.int32)
    for c in range(8):
        count = jnp.where(cell == c, count_ref[c // 4, c // 2 % 2, c % 2], count)
    live = lane < count
    kinds = kinds_ref[...]
    sigma = jnp.broadcast_to(sigma_ref[...] * (0.5 * UNIT), (8, 128))
    depth = jnp.broadcast_to(jnp.sqrt(eps_ref[...]) * DEPTH_UNIT, (8, 128))
    sigma = jnp.take_along_axis(sigma, kinds, axis=1, mode="promise_in_bounds")
    depth = jnp.take_along_axis(depth, kinds, axis=1, mode="promise_in_bounds")

    cells = codes_ref[0:1, :]
    codes = codes_ref[1:2, :]
    width = codes_ref.shape[1]
    is_cell = lax.broadcasted_iota(jnp.int32, (8, width), 0) == cells
    is_code = lax.broadcasted_iota(jnp.int32, (128, width), 0) == codes
    listed = lax.dot_general(
        jnp.where(is_cell, 1.0, 0.0).astype(jnp.bfloat16),
        jnp.where(is_code, 1.0, 0.0).astype(jnp.bfloat16),
        (((1,), (1,)), ((), ())),
        preferred_element_type=jnp.float32,
    )
    meta = jnp.where(lane == COUNT_LANE, count.astype(jnp.float32), listed)

    values = [rows_ref[0] * UNIT, rows_ref[1] * UNIT, rows_ref[2] * UNIT]
    values.append(jnp.where(live, rows_ref[3] * CHARGE_UNIT, 0.0))
    values.append(jnp.where(live, sigma, 0.5 * UNIT))
    values.append(jnp.where(live, depth, 0.0))
    values += [meta, jnp.zeros((8, 128), jnp.float32)]
    for r in range(8):
        own_ref[:, r, :] = values[r]

    odd = parities()
    toward = [1 - b for b in odd]
    for rel in RELATIONS:
        slot = sum(lax.bitwise_xor(odd[a], rel[a]) * (4, 2, 1)[a] for a in range(3))
        for n, (x, y, z) in enumerate(free_cells(rel, toward, 2)):
            send_ref[slot, n] = own_ref[4 * x + 2 * y + z]


def relay_kernel(own_ref, got_ref, send_ref):
    odd = parities()
    for rel in RELATIONS:
        slot = sum(lax.bitwise_xor(1 - odd[a], rel[a]) * (4, 2, 1)[a] for a in range(3))
        for n, at in enumerate(free_cells(rel, odd, 3)):
            far = [isinstance(p, int) and p == 2 for p in at]
            if not any(far):
                send_ref[slot, n] = own_ref[4 * at[0] + 2 * at[1] + at[2]]
                continue
            source = sum(lax.bitwise_xor(odd[a], int(far[a])) * (4, 2, 1)[a] for a in range(3))
            m = 0
            for a in range(3):
                if not far[a]:
                    m = m * 2 + at[a]
            send_ref[slot, n] = got_ref[source, m]


def place(ext_ref, meta_ref, own_ref, even_ref, odd_ref):
    odd = parities()
    spot = [[1, 2, 3 - 3 * odd[a], 3 * odd[a]] for a in range(3)]

    def put(at, tile):
        where = spot[0][at[0]] * 16 + spot[1][at[1]] * 4 + spot[2][at[2]]
        ext_ref[where] = tile
        meta_ref[pl.ds(where, 1), :] = tile[META_ROW:META_ROW + 1, :].astype(jnp.int32)

    for c in range(8):
        put((c // 4, c // 2 % 2, c % 2), own_ref[c])
    for rel in RELATIONS:
        slot = sum(lax.bitwise_xor(odd[a], rel[a]) * (4, 2, 1)[a] for a in range(3))
        for n, at in enumerate(free_cells(rel, (2, 2, 2), 2)):
            put(at, even_ref[slot, n])
        slot = sum(lax.bitwise_xor(1 - odd[a], rel[a]) * (4, 2, 1)[a] for a in range(3))
        for n, at in enumerate(free_cells(rel, (3, 3, 3), 3)):
            put(at, odd_ref[slot, n])


def pair_terms(home, other):
    dx = home[0] - other[0]
    dy = home[1] - other[1]
    dz = home[2] - other[2]
    dist = dx * dx + dy * dy + dz * dz
    size = home[4] + other[4]
    size = size * size
    root = lax.rsqrt(dist + size)
    inverse = root * root
    ratio = size * inverse
    cube = ratio * ratio * ratio
    coulomb = home[3] * other[3] * root
    attract = home[5] * other[5] * cube
    repel = attract * cube
    core = repel - attract
    energy = core + 6.0 * coulomb
    slope = core + repel + coulomb
    inner = jnp.clip(CUT / WIDTH - dist, 0.0, 1.0)
    scale = inner * ((1.0 - inner) * energy + (inner * (1.5 - inner)) * inverse * slope)
    return scale * dx, scale * dy, scale * dz


def force_kernel(own_ref, even_ref, odd_ref, out_ref, ext_ref, meta_ref, info_ref, list_ref, cols_ref, sums_ref, rows_ref, sem):
    place(ext_ref, meta_ref, own_ref, even_ref, odd_ref)
    copy = pltpu.make_async_copy(meta_ref, info_ref, sem)
    copy.start()
    copy.wait()
    lane = lax.broadcasted_iota(jnp.int32, (8, 128), 1)
    row = lax.broadcasted_iota(jnp.int32, (8, 128), 0)
    filler = jnp.where(row < 3, 100.0, jnp.where(row == 4, 0.5 * UNIT, 0.0))

    def shift(move):
        vector = jnp.zeros((8, 128), jnp.float32)
        for a in range(3):
            if move[a]:
                vector = jnp.where(row == a, move[a] * EDGE, vector)
        return vector

    def cell_step(c, carry):
        here = (1 + c // 4) * 16 + (1 + c // 2 % 2) * 4 + 1 + c % 2
        atoms = info_ref[here, COUNT_LANE]
        end = jnp.int32(0)
        current = filler
        for code in range(27):
            move = (code // 9 - 1, code // 3 % 3 - 1, code % 3 - 1)
            there = here + move[0] * 16 + move[1] * 4 + move[2]
            listed = info_ref[here, code] + info_ref[there, 26 - code]
            size = jnp.where(listed > 0, info_ref[there, COUNT_LANE], 0)
            chunk = lax.shift_right_logical(end, 7)
            first = lax.bitwise_and(end, 127)
            tile = pltpu.roll(ext_ref[there] + shift(move), first, axis=1)
            merged = jnp.where(lane < first, current, tile)
            list_ref[chunk] = merged
            end = end + size
            current = jnp.where(lax.shift_right_logical(end, 7) > chunk, tile, merged)
        chunk = lax.shift_right_logical(end, 7)
        list_ref[chunk] = jnp.where(lane < lax.bitwise_and(end, 127), current, filler)
        list_ref[chunk + 1] = filler
        rounds = lax.shift_right_logical(end + 255, 8)
        cols_ref[...] = jnp.transpose(ext_ref[here])
        sums_ref[...] = jnp.zeros(sums_ref.shape, jnp.float32)

        def group_step(g, carry):
            first = pl.multiple_of(g * 16, 16)
            homes = []
            for h in range(2):
                cols = cols_ref[pl.ds(first + 8 * h, 8), :]
                homes.append([jnp.broadcast_to(cols[:, r:r + 1], (8, 128)) for r in range(6)])

            def chunk_step(k, sums):
                sums = list(sums)
                for u in range(2):
                    other = [jnp.broadcast_to(list_ref[2 * k + u, r:r + 1, :], (8, 128)) for r in range(6)]
                    for h in range(2):
                        terms = pair_terms(homes[h], other)
                        for a in range(3):
                            sums[3 * h + a] = sums[3 * h + a] + terms[a]
                return tuple(sums)

            sums = lax.fori_loop(0, rounds, chunk_step, (jnp.zeros((8, 128), jnp.float32),) * 6)
            for h in range(2):
                total = [jnp.sum(sums[3 * h + a], axis=1, keepdims=True) for a in range(3)]
                line = jnp.where(lane == 0, total[0], jnp.where(lane == 1, total[1], total[2]))
                sums_ref[pl.ds(first + 8 * h, 8), :] = line[:, 0:8]
            return carry

        lax.fori_loop(0, lax.shift_right_logical(atoms + 15, 4), group_step, 0)
        rows_ref[c] = jnp.transpose(sums_ref[...]) * FORCE_UNIT
        return carry

    lax.fori_loop(0, 8, cell_step, 0)
    for c in range(8):
        for a in range(3):
            out_ref[a, c // 4, c // 2 % 2, c % 2:c % 2 + 1, :] = rows_ref[c, a:a + 1, :]


def swap_groups(sizes, start):
    def index(x, y, z):
        return ((x % sizes[0]) * sizes[1] + y % sizes[1]) * sizes[2] + z % sizes[2]

    bits = [(b // 4, b // 2 % 2, b % 2) for b in range(8)]
    return [
        [index(x + start + bx, y + start + by, z + start + bz) for bx, by, bz in bits]
        for x in range(0, sizes[0], 2)
        for y in range(0, sizes[1], 2)
        for z in range(0, sizes[2], 2)
    ]


def per_device(positions, charges, atom_types, atom_counts, type_sigma, type_epsilon, pair_list):
    f32 = jnp.float32
    sizes = [lax.axis_size(name) for name in AXES]
    vmem = pl.BlockSpec(memory_space=pltpu.VMEM)
    smem = pl.BlockSpec(memory_space=pltpu.SMEM)
    own, send = pl.pallas_call(
        atoms_kernel,
        out_shape=(jax.ShapeDtypeStruct((8, 8, 128), f32), jax.ShapeDtypeStruct((8, 4, 8, 128), f32)),
        in_specs=[vmem, vmem, vmem, smem, vmem, vmem, vmem],
        out_specs=(vmem, vmem),
        scratch_shapes=[pltpu.VMEM((4, 8, 128), f32), pltpu.VMEM((8, 128), jnp.int32), pltpu.VMEM((8, 256), jnp.int32)],
        name="atoms",
    )(positions, charges, atom_types, atom_counts, type_sigma.reshape(1, -1), type_epsilon.reshape(1, -1), pair_list)
    even = lax.all_to_all(send, AXES, 0, 0, axis_index_groups=swap_groups(sizes, 0), tiled=True)
    send = pl.pallas_call(
        relay_kernel,
        out_shape=jax.ShapeDtypeStruct((8, 9, 8, 128), f32),
        in_specs=[vmem, vmem],
        out_specs=vmem,
        name="relay",
    )(own, even)
    odd = lax.all_to_all(send, AXES, 0, 0, axis_index_groups=swap_groups(sizes, 1), tiled=True)
    return pl.pallas_call(
        force_kernel,
        out_shape=jax.ShapeDtypeStruct((3, 2, 2, 2, 128), f32),
        in_specs=[vmem, vmem, vmem],
        out_specs=vmem,
        scratch_shapes=[
            pltpu.VMEM((64, 8, 128), f32),
            pltpu.VMEM((64, 128), jnp.int32),
            pltpu.SMEM((64, 128), jnp.int32),
            pltpu.VMEM((MAX_CHUNKS, 8, 128), f32),
            pltpu.VMEM((128, 8), f32),
            pltpu.VMEM((128, 8), f32),
            pltpu.VMEM((8, 8, 128), f32),
            pltpu.SemaphoreType.DMA(()),
        ],
        name="forces",
    )(own, even, odd)


def solution(mesh):
    placed = (
        P(None, "gx", "gy", "gz", None),
        P("gx", "gy", "gz", None),
        P("gx", "gy", "gz", None),
        P("gx", "gy", "gz"),
        P(),
        P(),
        P(None, "gx", "gy", "gz", None),
    )
    return jax.shard_map(
        per_device,
        mesh=mesh,
        in_specs=placed,
        out_specs=P(None, "gx", "gy", "gz", None),
        check_vma=False,
    )
```

```python
import math

import jax
import jax.numpy as jnp
from jax import lax
from jax.experimental import pallas as pl
from jax.experimental.pallas import tpu as pltpu
from jax.sharding import PartitionSpec as P

AXES = ("gx", "gy", "gz")
CUT = 144.0
WIDTH = 44.0
UNIT = 1.0 / math.sqrt(WIDTH)
EDGE = 12.0 * UNIT
CHARGE_UNIT = WIDTH ** -0.25
DEPTH_UNIT = math.sqrt(24.0)
FORCE_UNIT = 2.0 / WIDTH * math.sqrt(WIDTH)
COUNT_LANE = 27
DONE_LANE = 28
META_ROW = 6
RELATIONS = [(r // 4, r // 2 % 2, r % 2) for r in range(1, 8)]
MAX_CHUNKS = 32


def parities():
    return [lax.rem(lax.axis_index(name), 2) for name in AXES]


def early_stages():
    x, y, z = [lax.axis_index(name) for name in AXES]
    last = lax.axis_size("gy") - 1
    corner = jnp.maximum(x, jnp.maximum(y, z)) < 2
    beside = jnp.logical_and(x < 3, jnp.logical_or(y < 3, y == last))
    first = jnp.logical_and(corner, x + y + z > 0)
    second = jnp.logical_and(jnp.logical_or(x == 0, beside), jnp.logical_not(corner))
    return first, second


def free_cells(relation, fixed, choices):
    spans = [[fixed[a]] if relation[a] else list(range(choices)) for a in range(3)]
    return [(x, y, z) for x in spans[0] for y in spans[1] for z in spans[2]]


def atoms_kernel(pos_ref, charge_ref, type_ref, count_ref, sigma_ref, eps_ref, pair_ref, own_ref, send_ref, part_ref, rows_ref, kinds_ref, codes_ref, *work):
    for i in range(2):
        for j in range(2):
            at = pl.ds(4 * i + 2 * j, 2)
            for comp in range(3):
                rows_ref[comp, at, :] = pos_ref[comp, i, j]
            rows_ref[3, at, :] = charge_ref[i, j]
            kinds_ref[at, :] = type_ref[i, j]
    codes_ref[...] = jnp.full(codes_ref.shape, -1, jnp.int32)
    slots = pair_ref.shape[-1]
    codes_ref[0:1, 0:slots] = pair_ref[0, 0, 0]
    codes_ref[1:2, 0:slots] = pair_ref[1, 0, 0]

    cell = lax.broadcasted_iota(jnp.int32, (8, 128), 0)
    lane = lax.broadcasted_iota(jnp.int32, (8, 128), 1)
    count = jnp.zeros((8, 128), jnp.int32)
    for c in range(8):
        count = jnp.where(cell == c, count_ref[c // 4, c // 2 % 2, c % 2], count)
    live = lane < count
    kinds = kinds_ref[...]
    sigma = jnp.broadcast_to(sigma_ref[...] * (0.5 * UNIT), (8, 128))
    depth = jnp.broadcast_to(jnp.sqrt(eps_ref[...]) * DEPTH_UNIT, (8, 128))
    sigma = jnp.take_along_axis(sigma, kinds, axis=1, mode="promise_in_bounds")
    depth = jnp.take_along_axis(depth, kinds, axis=1, mode="promise_in_bounds")

    cells = codes_ref[0:1, :]
    codes = codes_ref[1:2, :]
    width = codes_ref.shape[1]
    is_cell = lax.broadcasted_iota(jnp.int32, (8, width), 0) == cells
    is_code = lax.broadcasted_iota(jnp.int32, (128, width), 0) == codes
    listed = lax.dot_general(
        jnp.where(is_cell, 1.0, 0.0).astype(jnp.bfloat16),
        jnp.where(is_code, 1.0, 0.0).astype(jnp.bfloat16),
        (((1,), (1,)), ((), ())),
        preferred_element_type=jnp.float32,
    )
    meta = jnp.where(lane == COUNT_LANE, count.astype(jnp.float32), listed)

    values = [rows_ref[0] * UNIT, rows_ref[1] * UNIT, rows_ref[2] * UNIT]
    values.append(jnp.where(live, rows_ref[3] * CHARGE_UNIT, 0.0))
    values.append(jnp.where(live, sigma, 0.5 * UNIT))
    values.append(jnp.where(live, depth, 0.0))
    values += [meta, jnp.zeros((8, 128), jnp.float32)]
    for r in range(8):
        own_ref[:, r, :] = values[r]

    odd = parities()
    toward = [1 - b for b in odd]
    for rel in RELATIONS:
        slot = sum(lax.bitwise_xor(odd[a], rel[a]) * (4, 2, 1)[a] for a in range(3))
        for n, (x, y, z) in enumerate(free_cells(rel, toward, 2)):
            send_ref[slot, n] = own_ref[4 * x + 2 * y + z]
    part_ref[...] = jnp.zeros(part_ref.shape, jnp.float32)

    @pl.when(early_stages()[0])
    def _():
        work[1][...] = jnp.zeros(work[1].shape, jnp.int32)
        place(work[0], work[1], odd, own_ref, None, None)
        cell_forces(part_ref, None, *work)


def relay_kernel(own_ref, got_ref, before_ref, send_ref, part_ref, *work):
    odd = parities()
    for rel in RELATIONS:
        slot = sum(lax.bitwise_xor(1 - odd[a], rel[a]) * (4, 2, 1)[a] for a in range(3))
        for n, at in enumerate(free_cells(rel, odd, 3)):
            far = [isinstance(p, int) and p == 2 for p in at]
            if not any(far):
                send_ref[slot, n] = own_ref[4 * at[0] + 2 * at[1] + at[2]]
                continue
            source = sum(lax.bitwise_xor(odd[a], int(far[a])) * (4, 2, 1)[a] for a in range(3))
            m = 0
            for a in range(3):
                if not far[a]:
                    m = m * 2 + at[a]
            send_ref[slot, n] = got_ref[source, m]
    part_ref[...] = before_ref[...]

    @pl.when(early_stages()[1])
    def _():
        work[1][...] = jnp.zeros(work[1].shape, jnp.int32)
        place(work[0], work[1], odd, own_ref, got_ref, None)
        cell_forces(part_ref, None, *work)


def place(ext_ref, meta_ref, odd, own_ref, even_ref, odd_ref, own_done=0, even_done=0):
    spot = [[1, 2, 3 - 3 * odd[a], 3 * odd[a]] for a in range(3)]
    lane = lax.broadcasted_iota(jnp.int32, (1, 128), 1)

    def put(at, tile, done):
        where = spot[0][at[0]] * 16 + spot[1][at[1]] * 4 + spot[2][at[2]]
        ext_ref[where] = tile
        meta = tile[META_ROW:META_ROW + 1, :].astype(jnp.int32)
        meta_ref[pl.ds(where, 1), :] = jnp.where(lane == DONE_LANE, done, meta)

    for c in range(8):
        put((c // 4, c // 2 % 2, c % 2), own_ref[c], own_done)
    for rel in RELATIONS:
        if even_ref is not None:
            slot = sum(lax.bitwise_xor(odd[a], rel[a]) * (4, 2, 1)[a] for a in range(3))
            for n, at in enumerate(free_cells(rel, (2, 2, 2), 2)):
                put(at, even_ref[slot, n], even_done)
        if odd_ref is not None:
            slot = sum(lax.bitwise_xor(1 - odd[a], rel[a]) * (4, 2, 1)[a] for a in range(3))
            for n, at in enumerate(free_cells(rel, (3, 3, 3), 3)):
                put(at, odd_ref[slot, n], 0)


def pair_terms(home, other):
    dx = home[0] - other[0]
    dy = home[1] - other[1]
    dz = home[2] - other[2]
    dist = dx * dx + dy * dy + dz * dz
    size = home[4] + other[4]
    size = size * size
    root = lax.rsqrt(dist + size)
    inverse = root * root
    ratio = size * inverse
    cube = ratio * ratio * ratio
    coulomb = home[3] * other[3] * root
    attract = home[5] * other[5] * cube
    repel = attract * cube
    core = repel - attract
    energy = core + 6.0 * coulomb
    slope = core + repel + coulomb
    inner = jnp.clip(CUT / WIDTH - dist, 0.0, 1.0)
    scale = inner * ((1.0 - inner) * energy + (inner * (1.5 - inner)) * inverse * slope)
    return scale * dx, scale * dy, scale * dz


WORK = [
    pltpu.VMEM((64, 8, 128), jnp.float32),
    pltpu.VMEM((64, 128), jnp.int32),
    pltpu.SMEM((64, 128), jnp.int32),
    pltpu.VMEM((MAX_CHUNKS, 8, 128), jnp.float32),
    pltpu.VMEM((6, 128, 128), jnp.float32),
    pltpu.VMEM((8, 3, 128, 128), jnp.float32),
    pltpu.SemaphoreType.DMA(()),
]


def cell_forces(rows_ref, before_ref, ext_ref, meta_ref, info_ref, list_ref, home_ref, sums_ref, sem):
    copy = pltpu.make_async_copy(meta_ref, info_ref, sem)
    copy.start()
    copy.wait()
    lane = lax.broadcasted_iota(jnp.int32, (8, 128), 1)
    row = lax.broadcasted_iota(jnp.int32, (8, 128), 0)
    filler = jnp.where(row < 3, 100.0, jnp.where(row == 4, 0.5 * UNIT, 0.0))

    def shift(move):
        vector = jnp.zeros((8, 128), jnp.float32)
        for a in range(3):
            if move[a]:
                vector = jnp.where(row == a, move[a] * EDGE, vector)
        return vector

    def cell_step(c, carry):
        here = (1 + c // 4) * 16 + (1 + c // 2 % 2) * 4 + 1 + c % 2
        atoms = info_ref[here, COUNT_LANE]
        end = jnp.int32(0)
        current = filler
        for code in range(27):
            move = (code // 9 - 1, code // 3 % 3 - 1, code % 3 - 1)
            there = here + move[0] * 16 + move[1] * 4 + move[2]
            listed = info_ref[here, code] + info_ref[there, 26 - code] > 2 * info_ref[there, DONE_LANE]
            size = jnp.where(listed, info_ref[there, COUNT_LANE], 0)
            chunk = lax.shift_right_logical(end, 7)
            first = lax.bitwise_and(end, 127)
            tile = pltpu.roll(ext_ref[there] + shift(move), first, axis=1)
            merged = jnp.where(lane < first, current, tile)
            list_ref[chunk] = merged
            end = end + size
            current = jnp.where(lax.shift_right_logical(end, 7) > chunk, tile, merged)
        chunk = lax.shift_right_logical(end, 7)
        list_ref[chunk] = jnp.where(lane < lax.bitwise_and(end, 127), current, filler)
        list_ref[chunk + 1] = filler
        pairs = lax.shift_right_logical(end + 255, 8)
        cols = jnp.transpose(ext_ref[here])
        for r in range(6):
            home_ref[r] = jnp.broadcast_to(cols[:, r:r + 1], (128, 128))
        sums_ref[c] = jnp.zeros(sums_ref.shape[1:], jnp.float32)

        def group_step(g, carry):
            first = pl.multiple_of(g * 16, 16)
            homes = []
            for h in range(2):
                homes.append([home_ref[r, pl.ds(first + 8 * h, 8), :] for r in range(6)])

            def chunk_step(start, width, sums):
                sums = list(sums)
                for u in range(width):
                    other = [jnp.broadcast_to(list_ref[start + u, r:r + 1, :], (8, 128)) for r in range(6)]
                    for h in range(2):
                        terms = pair_terms(homes[h], other)
                        for a in range(3):
                            sums[3 * h + a] = sums[3 * h + a] + terms[a]
                return tuple(sums)

            fours = lax.shift_right_logical(pairs, 1)
            sums = (jnp.zeros((8, 128), jnp.float32),) * 6
            sums = lax.fori_loop(0, fours, lambda k, x: chunk_step(4 * k, 4, x), sums)
            sums = lax.fori_loop(2 * fours, pairs, lambda k, x: chunk_step(2 * k, 2, x), sums)
            for h in range(2):
                for a in range(3):
                    sums_ref[c, a, pl.ds(first + 8 * h, 8), :] = sums[3 * h + a]
            return carry

        lax.fori_loop(0, lax.shift_right_logical(atoms + 15, 4), group_step, 0)
        return carry

    lax.fori_loop(0, 8, cell_step, 0)
    comp = lax.broadcasted_iota(jnp.int32, (128, 8), 1)
    for c in range(8):
        total = [jnp.sum(sums_ref[c, a], axis=1, keepdims=True) for a in range(3)]
        line = jnp.where(comp == 0, total[0], jnp.where(comp == 1, total[1], total[2]))
        rows = jnp.transpose(line)
        rows_ref[c] = rows if before_ref is None else rows + before_ref[c]


def force_kernel(own_ref, even_ref, odd_ref, before_ref, out_ref, rows_ref, *work):
    first, second = early_stages()
    own_done = jnp.where(jnp.logical_or(first, second), 1, 0)
    place(work[0], work[1], parities(), own_ref, even_ref, odd_ref, own_done, jnp.where(second, 1, 0))
    cell_forces(rows_ref, before_ref, *work)
    for c in range(8):
        for a in range(3):
            out_ref[a, c // 4, c // 2 % 2, c % 2:c % 2 + 1, :] = rows_ref[c, a:a + 1, :] * FORCE_UNIT


def swap_groups(sizes, start):
    def index(x, y, z):
        return ((x % sizes[0]) * sizes[1] + y % sizes[1]) * sizes[2] + z % sizes[2]

    bits = [(b // 4, b // 2 % 2, b % 2) for b in range(8)]
    return [
        [index(x + start + bx, y + start + by, z + start + bz) for bx, by, bz in bits]
        for x in range(0, sizes[0], 2)
        for y in range(0, sizes[1], 2)
        for z in range(0, sizes[2], 2)
    ]


def per_device(positions, charges, atom_types, atom_counts, type_sigma, type_epsilon, pair_list):
    f32 = jnp.float32
    sizes = [lax.axis_size(name) for name in AXES]
    vmem = pl.BlockSpec(memory_space=pltpu.VMEM)
    smem = pl.BlockSpec(memory_space=pltpu.SMEM)
    part_shape = jax.ShapeDtypeStruct((8, 8, 128), f32)
    own, send, part = pl.pallas_call(
        atoms_kernel,
        out_shape=(part_shape, jax.ShapeDtypeStruct((8, 4, 8, 128), f32), part_shape),
        in_specs=[vmem, vmem, vmem, smem, vmem, vmem, vmem],
        out_specs=(vmem, vmem, vmem),
        scratch_shapes=[pltpu.VMEM((4, 8, 128), f32), pltpu.VMEM((8, 128), jnp.int32), pltpu.VMEM((8, 256), jnp.int32)] + WORK,
        name="atoms",
    )(positions, charges, atom_types, atom_counts, type_sigma.reshape(1, -1), type_epsilon.reshape(1, -1), pair_list)
    even = lax.all_to_all(send, AXES, 0, 0, axis_index_groups=swap_groups(sizes, 0), tiled=True)
    send, part = pl.pallas_call(
        relay_kernel,
        out_shape=(jax.ShapeDtypeStruct((8, 9, 8, 128), f32), part_shape),
        in_specs=[vmem, vmem, vmem],
        out_specs=(vmem, vmem),
        scratch_shapes=WORK,
        name="relay",
    )(own, even, part)
    odd = lax.all_to_all(send, AXES, 0, 0, axis_index_groups=swap_groups(sizes, 1), tiled=True)
    return pl.pallas_call(
        force_kernel,
        out_shape=jax.ShapeDtypeStruct((3, 2, 2, 2, 128), f32),
        in_specs=[vmem] * 4,
        out_specs=vmem,
        scratch_shapes=[pltpu.VMEM((8, 8, 128), f32)] + WORK,
        name="forces",
    )(own, even, odd, part)


def solution(mesh):
    placed = (
        P(None, "gx", "gy", "gz", None),
        P("gx", "gy", "gz", None),
        P("gx", "gy", "gz", None),
        P("gx", "gy", "gz"),
        P(),
        P(),
        P(None, "gx", "gy", "gz", None),
    )
    return jax.shard_map(
        per_device,
        mesh=mesh,
        in_specs=placed,
        out_specs=P(None, "gx", "gy", "gz", None),
        check_vma=False,
    )
```

```python
import math

import jax
import jax.numpy as jnp
from jax import lax
from jax.experimental import pallas as pl
from jax.experimental.pallas import tpu as pltpu
from jax.sharding import PartitionSpec as P

AXES = ("gx", "gy", "gz")
CUT = 144.0
WIDTH = 44.0
UNIT = 1.0 / math.sqrt(WIDTH)
EDGE = 12.0 * UNIT
CHARGE_UNIT = WIDTH ** -0.25
DEPTH_UNIT = math.sqrt(24.0)
FORCE_UNIT = 2.0 / WIDTH * math.sqrt(WIDTH)
COUNT_LANE = 27
DONE_LANE = 28
META_ROW = 6
RELATIONS = [(r // 4, r // 2 % 2, r % 2) for r in range(1, 8)]
MAX_CHUNKS = 32


def parities():
    return [lax.rem(lax.axis_index(name), 2) for name in AXES]


def early_stages():
    x, y, z = [lax.axis_index(name) for name in AXES]
    last = lax.axis_size("gy") - 1
    corner = jnp.maximum(x, jnp.maximum(y, z)) < 2
    beside = jnp.logical_and(x < 3, jnp.logical_or(y < 3, y == last))
    first = jnp.logical_and(corner, x + y + z > 0)
    second = jnp.logical_and(jnp.logical_or(x == 0, beside), jnp.logical_not(corner))
    return first, second


def free_cells(relation, fixed, choices):
    spans = [[fixed[a]] if relation[a] else list(range(choices)) for a in range(3)]
    return [(x, y, z) for x in spans[0] for y in spans[1] for z in spans[2]]


def atoms_kernel(pos_ref, charge_ref, type_ref, count_ref, sigma_ref, eps_ref, pair_ref, own_ref, send_ref, part_ref, rows_ref, kinds_ref, codes_ref, *work):
    for i in range(2):
        for j in range(2):
            at = pl.ds(4 * i + 2 * j, 2)
            for comp in range(3):
                rows_ref[comp, at, :] = pos_ref[comp, i, j]
            rows_ref[3, at, :] = charge_ref[i, j]
            kinds_ref[at, :] = type_ref[i, j]
    codes_ref[...] = jnp.full(codes_ref.shape, -1, jnp.int32)
    slots = pair_ref.shape[-1]
    codes_ref[0:1, 0:slots] = pair_ref[0, 0, 0]
    codes_ref[1:2, 0:slots] = pair_ref[1, 0, 0]

    cell = lax.broadcasted_iota(jnp.int32, (8, 128), 0)
    lane = lax.broadcasted_iota(jnp.int32, (8, 128), 1)
    count = jnp.zeros((8, 128), jnp.int32)
    for c in range(8):
        count = jnp.where(cell == c, count_ref[c // 4, c // 2 % 2, c % 2], count)
    live = lane < count
    kinds = kinds_ref[...]
    sigma = jnp.broadcast_to(sigma_ref[...] * (0.5 * UNIT), (8, 128))
    depth = jnp.broadcast_to(jnp.sqrt(eps_ref[...]) * DEPTH_UNIT, (8, 128))
    sigma = jnp.take_along_axis(sigma, kinds, axis=1, mode="promise_in_bounds")
    depth = jnp.take_along_axis(depth, kinds, axis=1, mode="promise_in_bounds")

    cells = codes_ref[0:1, :]
    codes = codes_ref[1:2, :]
    width = codes_ref.shape[1]
    is_cell = lax.broadcasted_iota(jnp.int32, (8, width), 0) == cells
    is_code = lax.broadcasted_iota(jnp.int32, (128, width), 0) == codes
    listed = lax.dot_general(
        jnp.where(is_cell, 1.0, 0.0).astype(jnp.bfloat16),
        jnp.where(is_code, 1.0, 0.0).astype(jnp.bfloat16),
        (((1,), (1,)), ((), ())),
        preferred_element_type=jnp.float32,
    )
    meta = jnp.where(lane == COUNT_LANE, count.astype(jnp.float32), listed)

    values = [rows_ref[0] * UNIT, rows_ref[1] * UNIT, rows_ref[2] * UNIT]
    values.append(jnp.where(live, rows_ref[3] * CHARGE_UNIT, 0.0))
    values.append(jnp.where(live, sigma, 0.5 * UNIT))
    values.append(jnp.where(live, depth, 0.0))
    values += [meta, jnp.zeros((8, 128), jnp.float32)]
    for r in range(8):
        own_ref[:, r, :] = values[r]

    odd = parities()
    toward = [1 - b for b in odd]
    for rel in RELATIONS:
        slot = sum(lax.bitwise_xor(odd[a], rel[a]) * (4, 2, 1)[a] for a in range(3))
        for n, (x, y, z) in enumerate(free_cells(rel, toward, 2)):
            send_ref[slot, n] = own_ref[4 * x + 2 * y + z]
    part_ref[...] = jnp.zeros(part_ref.shape, jnp.float32)

    @pl.when(early_stages()[0])
    def _():
        work[1][...] = jnp.zeros(work[1].shape, jnp.int32)
        place(work[0], work[1], odd, own_ref, None, None)
        cell_forces(part_ref, None, *work)


def relay_kernel(own_ref, got_ref, before_ref, send_ref, part_ref, *work):
    odd = parities()
    for rel in RELATIONS:
        slot = sum(lax.bitwise_xor(1 - odd[a], rel[a]) * (4, 2, 1)[a] for a in range(3))
        for n, at in enumerate(free_cells(rel, odd, 3)):
            far = [isinstance(p, int) and p == 2 for p in at]
            if not any(far):
                send_ref[slot, n] = own_ref[4 * at[0] + 2 * at[1] + at[2]]
                continue
            source = sum(lax.bitwise_xor(odd[a], int(far[a])) * (4, 2, 1)[a] for a in range(3))
            m = 0
            for a in range(3):
                if not far[a]:
                    m = m * 2 + at[a]
            send_ref[slot, n] = got_ref[source, m]
    part_ref[...] = before_ref[...]

    @pl.when(early_stages()[1])
    def _():
        work[1][...] = jnp.zeros(work[1].shape, jnp.int32)
        place(work[0], work[1], odd, own_ref, got_ref, None)
        cell_forces(part_ref, None, *work)


def place(ext_ref, meta_ref, odd, own_ref, even_ref, odd_ref, own_done=0, even_done=0):
    spot = [[1, 2, 3 - 3 * odd[a], 3 * odd[a]] for a in range(3)]
    lane = lax.broadcasted_iota(jnp.int32, (1, 128), 1)

    def put(at, tile, done):
        where = spot[0][at[0]] * 16 + spot[1][at[1]] * 4 + spot[2][at[2]]
        ext_ref[where] = tile
        meta = tile[META_ROW:META_ROW + 1, :].astype(jnp.int32)
        meta_ref[pl.ds(where, 1), :] = jnp.where(lane == DONE_LANE, done, meta)

    for c in range(8):
        put((c // 4, c // 2 % 2, c % 2), own_ref[c], own_done)
    for rel in RELATIONS:
        if even_ref is not None:
            slot = sum(lax.bitwise_xor(odd[a], rel[a]) * (4, 2, 1)[a] for a in range(3))
            for n, at in enumerate(free_cells(rel, (2, 2, 2), 2)):
                put(at, even_ref[slot, n], even_done)
        if odd_ref is not None:
            slot = sum(lax.bitwise_xor(1 - odd[a], rel[a]) * (4, 2, 1)[a] for a in range(3))
            for n, at in enumerate(free_cells(rel, (3, 3, 3), 3)):
                put(at, odd_ref[slot, n], 0)


def pair_terms(home, other):
    dx = home[0] - other[0]
    dy = home[1] - other[1]
    dz = home[2] - other[2]
    dist = dx * dx + dy * dy + dz * dz
    size = home[4] + other[4]
    size = size * size
    root = lax.rsqrt(dist + size)
    inverse = root * root
    ratio = size * inverse
    cube = ratio * ratio * ratio
    coulomb = home[3] * other[3] * root
    attract = home[5] * other[5] * cube
    repel = attract * cube
    core = repel - attract
    energy = core + 6.0 * coulomb
    slope = core + repel + coulomb
    inner = jnp.clip(CUT / WIDTH - dist, 0.0, 1.0)
    scale = inner * ((1.0 - inner) * energy + (inner * (1.5 - inner)) * inverse * slope)
    return scale * dx, scale * dy, scale * dz


WORK = [
    pltpu.VMEM((64, 8, 128), jnp.float32),
    pltpu.VMEM((64, 128), jnp.int32),
    pltpu.SMEM((64, 128), jnp.int32),
    pltpu.VMEM((MAX_CHUNKS, 8, 128), jnp.float32),
    pltpu.VMEM((8, 6, 128, 128), jnp.float32),
    pltpu.VMEM((8, 3, 128, 128), jnp.float32),
    pltpu.SemaphoreType.DMA(()),
]


def cell_forces(rows_ref, before_ref, ext_ref, meta_ref, info_ref, list_ref, home_ref, sums_ref, sem):
    copy = pltpu.make_async_copy(meta_ref, info_ref, sem)
    copy.start()
    for c in range(8):
        cols = jnp.transpose(ext_ref[(1 + c // 4) * 16 + (1 + c // 2 % 2) * 4 + 1 + c % 2])
        for r in range(6):
            home_ref[c, r] = jnp.broadcast_to(cols[:, r:r + 1], (128, 128))
    copy.wait()
    lane = lax.broadcasted_iota(jnp.int32, (8, 128), 1)
    row = lax.broadcasted_iota(jnp.int32, (8, 128), 0)
    filler = jnp.where(row < 3, 100.0, jnp.where(row == 4, 0.5 * UNIT, 0.0))

    def shift(move):
        vector = jnp.zeros((8, 128), jnp.float32)
        for a in range(3):
            if move[a]:
                vector = jnp.where(row == a, move[a] * EDGE, vector)
        return vector

    def cell_step(c, carry):
        here = (1 + c // 4) * 16 + (1 + c // 2 % 2) * 4 + 1 + c % 2
        atoms = info_ref[here, COUNT_LANE]
        end = jnp.int32(0)
        current = filler
        for code in range(27):
            move = (code // 9 - 1, code // 3 % 3 - 1, code % 3 - 1)
            there = here + move[0] * 16 + move[1] * 4 + move[2]
            listed = info_ref[here, code] + info_ref[there, 26 - code] > 2 * info_ref[there, DONE_LANE]
            size = jnp.where(listed, info_ref[there, COUNT_LANE], 0)
            chunk = lax.shift_right_logical(end, 7)
            first = lax.bitwise_and(end, 127)
            tile = pltpu.roll(ext_ref[there] + shift(move), first, axis=1)
            merged = jnp.where(lane < first, current, tile)
            list_ref[chunk] = merged
            end = end + size
            current = jnp.where(lax.shift_right_logical(end, 7) > chunk, tile, merged)
        chunk = lax.shift_right_logical(end, 7)
        list_ref[chunk] = jnp.where(lane < lax.bitwise_and(end, 127), current, filler)
        list_ref[chunk + 1] = filler
        pairs = lax.shift_right_logical(end + 255, 8)

        def group_step(g, carry):
            first = pl.multiple_of(g * 16, 16)
            homes = []
            for h in range(2):
                homes.append([home_ref[c, r, pl.ds(first + 8 * h, 8), :] for r in range(6)])

            def chunk_step(start, width, sums):
                sums = list(sums)
                for u in range(width):
                    other = [jnp.broadcast_to(list_ref[start + u, r:r + 1, :], (8, 128)) for r in range(6)]
                    for h in range(2):
                        terms = pair_terms(homes[h], other)
                        for a in range(3):
                            sums[3 * h + a] = sums[3 * h + a] + terms[a]
                return tuple(sums)

            fours = lax.shift_right_logical(pairs, 1)
            sums = (jnp.zeros((8, 128), jnp.float32),) * 6
            sums = lax.fori_loop(0, fours, lambda k, x: chunk_step(4 * k, 4, x), sums)
            sums = lax.fori_loop(2 * fours, pairs, lambda k, x: chunk_step(2 * k, 2, x), sums)
            for h in range(2):
                for a in range(3):
                    sums_ref[c, a, pl.ds(first + 8 * h, 8), :] = sums[3 * h + a]
            return carry

        lax.fori_loop(0, lax.shift_right_logical(atoms + 15, 4), group_step, 0)
        return carry

    lax.fori_loop(0, 8, cell_step, 0)
    comp = lax.broadcasted_iota(jnp.int32, (128, 8), 1)
    for c in range(8):
        total = [jnp.sum(sums_ref[c, a], axis=1, keepdims=True) for a in range(3)]
        line = jnp.where(comp == 0, total[0], jnp.where(comp == 1, total[1], total[2]))
        atoms = info_ref[(1 + c // 4) * 16 + (1 + c // 2 % 2) * 4 + 1 + c % 2, COUNT_LANE]
        rows = jnp.where(lane < atoms, jnp.transpose(line), 0.0)
        rows_ref[c] = rows if before_ref is None else rows + before_ref[c]


def force_kernel(own_ref, even_ref, odd_ref, before_ref, out_ref, rows_ref, *work):
    first, second = early_stages()
    own_done = jnp.where(jnp.logical_or(first, second), 1, 0)
    place(work[0], work[1], parities(), own_ref, even_ref, odd_ref, own_done, jnp.where(second, 1, 0))
    cell_forces(rows_ref, before_ref, *work)
    for c in range(8):
        for a in range(3):
            out_ref[a, c // 4, c // 2 % 2, c % 2:c % 2 + 1, :] = rows_ref[c, a:a + 1, :] * FORCE_UNIT


def swap_groups(sizes, start):
    def index(x, y, z):
        return ((x % sizes[0]) * sizes[1] + y % sizes[1]) * sizes[2] + z % sizes[2]

    bits = [(b // 4, b // 2 % 2, b % 2) for b in range(8)]
    return [
        [index(x + start + bx, y + start + by, z + start + bz) for bx, by, bz in bits]
        for x in range(0, sizes[0], 2)
        for y in range(0, sizes[1], 2)
        for z in range(0, sizes[2], 2)
    ]


def per_device(positions, charges, atom_types, atom_counts, type_sigma, type_epsilon, pair_list):
    f32 = jnp.float32
    sizes = [lax.axis_size(name) for name in AXES]
    vmem = pl.BlockSpec(memory_space=pltpu.VMEM)
    smem = pl.BlockSpec(memory_space=pltpu.SMEM)
    part_shape = pltpu.VMEM((8, 8, 128), f32)
    keep = lambda x: pltpu.with_memory_space_constraint(x, pltpu.VMEM)
    own, send, part = pl.pallas_call(
        atoms_kernel,
        out_shape=(part_shape, pltpu.VMEM((8, 4, 8, 128), f32), part_shape),
        in_specs=[vmem, vmem, vmem, smem, vmem, vmem, vmem],
        out_specs=(vmem, vmem, vmem),
        scratch_shapes=[pltpu.VMEM((4, 8, 128), f32), pltpu.VMEM((8, 128), jnp.int32), pltpu.VMEM((8, 256), jnp.int32)] + WORK,
        name="atoms",
    )(positions, charges, atom_types, atom_counts, type_sigma.reshape(1, -1), type_epsilon.reshape(1, -1), pair_list)
    even = lax.all_to_all(send, AXES, 0, 0, axis_index_groups=swap_groups(sizes, 0), tiled=True)
    send, part = pl.pallas_call(
        relay_kernel,
        out_shape=(pltpu.VMEM((8, 9, 8, 128), f32), part_shape),
        in_specs=[vmem, vmem, vmem],
        out_specs=(vmem, vmem),
        scratch_shapes=WORK,
        name="relay",
    )(keep(own), keep(even), keep(part))
    odd = lax.all_to_all(send, AXES, 0, 0, axis_index_groups=swap_groups(sizes, 1), tiled=True)
    return pl.pallas_call(
        force_kernel,
        out_shape=jax.ShapeDtypeStruct((3, 2, 2, 2, 128), f32),
        in_specs=[vmem] * 4,
        out_specs=vmem,
        scratch_shapes=[pltpu.VMEM((8, 8, 128), f32)] + WORK,
        name="forces",
    )(keep(own), keep(even), keep(odd), keep(part))


def solution(mesh):
    placed = (
        P(None, "gx", "gy", "gz", None),
        P("gx", "gy", "gz", None),
        P("gx", "gy", "gz", None),
        P("gx", "gy", "gz"),
        P(),
        P(),
        P(None, "gx", "gy", "gz", None),
    )
    return jax.shard_map(
        per_device,
        mesh=mesh,
        in_specs=placed,
        out_specs=P(None, "gx", "gy", "gz", None),
        check_vma=False,
    )
```

```python
import math

import jax
import jax.numpy as jnp
from jax import lax
from jax.experimental import pallas as pl
from jax.experimental.pallas import tpu as pltpu
from jax.sharding import PartitionSpec as P

AXES = ("gx", "gy", "gz")
FIRST_PAIRS = (1, 0, 0)
CUT = 144.0
WIDTH = 44.0
UNIT = 1.0 / math.sqrt(WIDTH)
EDGE = 12.0 * UNIT
CHARGE_UNIT = WIDTH ** -0.25
DEPTH_UNIT = math.sqrt(24.0)
FORCE_UNIT = 2.0 / WIDTH * math.sqrt(WIDTH)
COUNT_LANE = 27
LEFT_LANE = 28
META_ROW = 6
RELATIONS = [(r // 4, r // 2 % 2, r % 2) for r in range(1, 8)]
MAX_CHUNKS = 32


def parities():
    return [lax.rem(lax.axis_index(name) + start, 2) for name, start in zip(AXES, FIRST_PAIRS)]


def early_stages():
    x, y, z = [lax.axis_index(name) for name in AXES]
    return jnp.logical_and(x == 0, y + z > 0), x == 1


def free_cells(relation, fixed, choices):
    spans = [[fixed[a]] if relation[a] else list(range(choices)) for a in range(3)]
    return [(x, y, z) for x in spans[0] for y in spans[1] for z in spans[2]]


def atoms_kernel(pos_ref, charge_ref, type_ref, count_ref, sigma_ref, eps_ref, pair_ref, own_ref, send_ref, part_ref, rows_ref, kinds_ref, codes_ref, *work):
    for i in range(2):
        for j in range(2):
            at = pl.ds(4 * i + 2 * j, 2)
            for comp in range(3):
                rows_ref[comp, at, :] = pos_ref[comp, i, j]
            rows_ref[3, at, :] = charge_ref[i, j]
            kinds_ref[at, :] = type_ref[i, j]
    codes_ref[...] = jnp.full(codes_ref.shape, -1, jnp.int32)
    slots = pair_ref.shape[-1]
    codes_ref[0:1, 0:slots] = pair_ref[0, 0, 0]
    codes_ref[1:2, 0:slots] = pair_ref[1, 0, 0]

    cell = lax.broadcasted_iota(jnp.int32, (8, 128), 0)
    lane = lax.broadcasted_iota(jnp.int32, (8, 128), 1)
    count = jnp.zeros((8, 128), jnp.int32)
    for c in range(8):
        count = jnp.where(cell == c, count_ref[c // 4, c // 2 % 2, c % 2], count)
    live = lane < count
    kinds = kinds_ref[...]
    sigma = jnp.broadcast_to(sigma_ref[...] * (0.5 * UNIT), (8, 128))
    depth = jnp.broadcast_to(jnp.sqrt(eps_ref[...]) * DEPTH_UNIT, (8, 128))
    sigma = jnp.take_along_axis(sigma, kinds, axis=1, mode="promise_in_bounds")
    depth = jnp.take_along_axis(depth, kinds, axis=1, mode="promise_in_bounds")

    cells = codes_ref[0:1, :]
    codes = codes_ref[1:2, :]
    width = codes_ref.shape[1]
    is_cell = lax.broadcasted_iota(jnp.int32, (8, width), 0) == cells
    is_code = lax.broadcasted_iota(jnp.int32, (128, width), 0) == codes
    listed = lax.dot_general(
        jnp.where(is_cell, 1.0, 0.0).astype(jnp.bfloat16),
        jnp.where(is_code, 1.0, 0.0).astype(jnp.bfloat16),
        (((1,), (1,)), ((), ())),
        preferred_element_type=jnp.float32,
    )
    atoms = count.astype(jnp.float32)
    meta = jnp.where(jnp.logical_or(lane == COUNT_LANE, lane == LEFT_LANE), atoms, listed * atoms)

    values = [rows_ref[0] * UNIT, rows_ref[1] * UNIT, rows_ref[2] * UNIT]
    values.append(jnp.where(live, rows_ref[3] * CHARGE_UNIT, 0.0))
    values.append(jnp.where(live, sigma, 0.5 * UNIT))
    values.append(jnp.where(live, depth, 0.0))
    values += [meta, jnp.zeros((8, 128), jnp.float32)]
    for r in range(8):
        own_ref[:, r, :] = values[r]

    odd = parities()
    toward = [1 - b for b in odd]
    for rel in RELATIONS:
        slot = sum(lax.bitwise_xor(odd[a], rel[a]) * (4, 2, 1)[a] for a in range(3))
        for n, (x, y, z) in enumerate(free_cells(rel, toward, 2)):
            send_ref[slot, n] = own_ref[4 * x + 2 * y + z]
    part_ref[...] = jnp.zeros(part_ref.shape, jnp.float32)

    @pl.when(early_stages()[0])
    def _():
        work[1][...] = jnp.zeros(work[1].shape, jnp.int32)
        place(work[0], work[1], odd, own_ref, None, None)
        cell_forces(part_ref, None, None, *work)


def relay_kernel(own_ref, got_ref, before_ref, send_ref, part_ref, *work):
    odd = parities()
    for rel in RELATIONS:
        slot = sum(lax.bitwise_xor(1 - odd[a], rel[a]) * (4, 2, 1)[a] for a in range(3))
        for n, at in enumerate(free_cells(rel, odd, 3)):
            far = [isinstance(p, int) and p == 2 for p in at]
            if not any(far):
                send_ref[slot, n] = own_ref[4 * at[0] + 2 * at[1] + at[2]]
                continue
            source = sum(lax.bitwise_xor(odd[a], int(far[a])) * (4, 2, 1)[a] for a in range(3))
            m = 0
            for a in range(3):
                if not far[a]:
                    m = m * 2 + at[a]
            send_ref[slot, n] = got_ref[source, m]
    part_ref[...] = before_ref[...]

    @pl.when(early_stages()[1])
    def _():
        work[1][...] = jnp.zeros(work[1].shape, jnp.int32)
        place(work[0], work[1], odd, own_ref, got_ref, None)
        cell_forces(part_ref, None, None, *work)


def place(ext_ref, meta_ref, odd, own_ref, even_ref, odd_ref, even_done=0):
    spot = [[1, 2, 3 - 3 * odd[a], 3 * odd[a]] for a in range(3)]
    lane = lax.broadcasted_iota(jnp.int32, (1, 128), 1)

    def put(at, tile, done):
        where = spot[0][at[0]] * 16 + spot[1][at[1]] * 4 + spot[2][at[2]]
        ext_ref[where] = tile
        meta = tile[META_ROW:META_ROW + 1, :].astype(jnp.int32)
        meta_ref[pl.ds(where, 1), :] = jnp.where(jnp.logical_and(lane != COUNT_LANE, done > 0), 0, meta)

    for c in range(8):
        put((c // 4, c // 2 % 2, c % 2), own_ref[c], 0)
    for rel in RELATIONS:
        if even_ref is not None:
            slot = sum(lax.bitwise_xor(odd[a], rel[a]) * (4, 2, 1)[a] for a in range(3))
            for n, at in enumerate(free_cells(rel, (2, 2, 2), 2)):
                put(at, even_ref[slot, n], even_done)
        if odd_ref is not None:
            slot = sum(lax.bitwise_xor(1 - odd[a], rel[a]) * (4, 2, 1)[a] for a in range(3))
            for n, at in enumerate(free_cells(rel, (3, 3, 3), 3)):
                put(at, odd_ref[slot, n], 0)


def pair_terms(home, other):
    dx = home[0] - other[0]
    dy = home[1] - other[1]
    dz = home[2] - other[2]
    dist = dx * dx + dy * dy + dz * dz
    size = home[4] + other[4]
    size = size * size
    root = lax.rsqrt(dist + size)
    inverse = root * root
    ratio = size * inverse
    cube = ratio * ratio * ratio
    coulomb = home[3] * other[3] * root
    attract = home[5] * other[5] * cube
    repel = attract * cube
    core = repel - attract
    energy = core + 6.0 * coulomb
    slope = core + repel + coulomb
    inner = jnp.clip(CUT / WIDTH - dist, 0.0, 1.0)
    scale = inner * ((1.0 - inner) * energy + (inner * (1.5 - inner)) * inverse * slope)
    return scale * dx, scale * dy, scale * dz


WORK = [
    pltpu.VMEM((64, 8, 128), jnp.float32),
    pltpu.VMEM((64, 128), jnp.int32),
    pltpu.SMEM((64, 128), jnp.int32),
    pltpu.VMEM((8, MAX_CHUNKS, 8, 128), jnp.float32),
    pltpu.SMEM((8,), jnp.int32),
    pltpu.VMEM((8, 6, 128, 128), jnp.float32),
    pltpu.VMEM((8, 3, 128, 128), jnp.float32),
    pltpu.SemaphoreType.DMA(()),
]


def spatial(c):
    return (1 + c // 4) * 16 + (1 + c // 2 % 2) * 4 + 1 + c % 2


def cell_forces(rows_ref, before_ref, own_done, ext_ref, meta_ref, info_ref, list_ref, pairs_ref, home_ref, sums_ref, sem):
    copy = pltpu.make_async_copy(meta_ref, info_ref, sem)
    copy.start()
    part = lax.broadcasted_iota(jnp.int32, (32, 768), 0)
    column = lax.broadcasted_iota(jnp.int32, (32, 768), 1)
    pick = jnp.logical_and(lax.bitwise_and(part, 7) == lax.shift_right_logical(column, 7), part < 24)
    pick = jnp.where(pick, 1.0, 0.0).astype(jnp.bfloat16)
    for c in range(8):
        rest = ext_ref[spatial(c)]
        pieces = []
        for _ in range(3):
            pieces.append(rest.astype(jnp.bfloat16).astype(jnp.float32))
            rest = rest - pieces[-1]
        pieces.append(jnp.zeros((8, 128), jnp.float32))
        cols = jnp.transpose(jnp.concatenate(pieces, 0)).astype(jnp.bfloat16)
        wide = lax.dot_general(cols, pick, (((1,), (0,)), ((), ())), preferred_element_type=jnp.float32)
        for r in range(6):
            home_ref[c, r] = wide[:, 128 * r:128 * (r + 1)]
    copy.wait()
    lane = lax.broadcasted_iota(jnp.int32, (8, 128), 1)
    row = lax.broadcasted_iota(jnp.int32, (8, 128), 0)
    filler = jnp.where(row < 3, 100.0, jnp.where(row == 4, 0.5 * UNIT, 0.0))

    def shift(move):
        vector = jnp.zeros((8, 128), jnp.float32)
        for a in range(3):
            if move[a]:
                vector = jnp.where(row == a, move[a] * EDGE, vector)
        return vector

    own_spots = [spatial(c) for c in range(8)]
    for c in range(8):
        here = spatial(c)
        end = jnp.int32(0)
        current = filler
        for code in range(27):
            move = (code // 9 - 1, code // 3 % 3 - 1, code % 3 - 1)
            there = here + move[0] * 16 + move[1] * 4 + move[2]
            size = jnp.where(info_ref[here, code] > 0, info_ref[there, LEFT_LANE], info_ref[there, 26 - code])
            if own_done is not None and there in own_spots:
                size = jnp.where(own_done, 0, size)
            chunk = lax.shift_right_logical(end, 7)
            first = lax.bitwise_and(end, 127)
            tile = pltpu.roll(ext_ref[there] + shift(move), first, axis=1)
            merged = jnp.where(lane < first, current, tile)
            list_ref[c, chunk] = merged
            end = end + size
            current = jnp.where(lax.shift_right_logical(end, 7) > chunk, tile, merged)
        chunk = lax.shift_right_logical(end, 7)
        list_ref[c, chunk] = jnp.where(lane < lax.bitwise_and(end, 127), current, filler)
        list_ref[c, chunk + 1] = filler
        pairs_ref[c] = lax.shift_right_logical(end + 255, 8)

    def cell_step(c, carry):
        here = (1 + c // 4) * 16 + (1 + c // 2 % 2) * 4 + 1 + c % 2
        atoms = info_ref[here, COUNT_LANE]
        pairs = pairs_ref[c]

        def group_step(g, carry):
            first = pl.multiple_of(g * 16, 16)
            homes = []
            for h in range(2):
                homes.append([home_ref[c, r, pl.ds(first + 8 * h, 8), :] for r in range(6)])

            def chunk_step(start, width, sums):
                sums = list(sums)
                for u in range(width):
                    other = [jnp.broadcast_to(list_ref[c, start + u, r:r + 1, :], (8, 128)) for r in range(6)]
                    for h in range(2):
                        terms = pair_terms(homes[h], other)
                        for a in range(3):
                            sums[3 * h + a] = sums[3 * h + a] + terms[a]
                return tuple(sums)

            fours = lax.shift_right_logical(pairs, 1)
            sums = (jnp.zeros((8, 128), jnp.float32),) * 6
            sums = lax.fori_loop(0, fours, lambda k, x: chunk_step(4 * k, 4, x), sums)
            sums = lax.fori_loop(2 * fours, pairs, lambda k, x: chunk_step(2 * k, 2, x), sums)
            for h in range(2):
                for a in range(3):
                    sums_ref[c, a, pl.ds(first + 8 * h, 8), :] = sums[3 * h + a]
            return carry

        lax.fori_loop(0, lax.shift_right_logical(atoms + 15, 4), group_step, 0)
        return carry

    lax.fori_loop(0, 8, cell_step, 0)
    comp = lax.broadcasted_iota(jnp.int32, (128, 8), 1)
    for c in range(8):
        total = [jnp.sum(sums_ref[c, a], axis=1, keepdims=True) for a in range(3)]
        line = jnp.where(comp == 0, total[0], jnp.where(comp == 1, total[1], total[2]))
        atoms = info_ref[spatial(c), COUNT_LANE]
        rows = jnp.where(lane < atoms, jnp.transpose(line), 0.0)
        rows_ref[c] = rows if before_ref is None else rows + before_ref[c]


def force_kernel(own_ref, even_ref, odd_ref, before_ref, out_ref, rows_ref, *work):
    first, second = early_stages()
    place(work[0], work[1], parities(), own_ref, even_ref, odd_ref, jnp.where(second, 1, 0))
    cell_forces(rows_ref, before_ref, jnp.logical_or(first, second), *work)
    for c in range(8):
        for a in range(3):
            out_ref[a, c // 4, c // 2 % 2, c % 2:c % 2 + 1, :] = rows_ref[c, a:a + 1, :] * FORCE_UNIT


def swap_groups(sizes, start):
    def index(x, y, z):
        return ((x % sizes[0]) * sizes[1] + y % sizes[1]) * sizes[2] + z % sizes[2]

    bits = [(b // 4, b // 2 % 2, b % 2) for b in range(8)]
    return [
        [index(x + start[0] + bx, y + start[1] + by, z + start[2] + bz) for bx, by, bz in bits]
        for x in range(0, sizes[0], 2)
        for y in range(0, sizes[1], 2)
        for z in range(0, sizes[2], 2)
    ]


def per_device(positions, charges, atom_types, atom_counts, type_sigma, type_epsilon, pair_list):
    f32 = jnp.float32
    sizes = [lax.axis_size(name) for name in AXES]
    vmem = pl.BlockSpec(memory_space=pltpu.VMEM)
    smem = pl.BlockSpec(memory_space=pltpu.SMEM)
    part_shape = pltpu.VMEM((8, 8, 128), f32)
    keep = lambda x: pltpu.with_memory_space_constraint(x, pltpu.VMEM)
    own, send, part = pl.pallas_call(
        atoms_kernel,
        out_shape=(part_shape, pltpu.VMEM((8, 4, 8, 128), f32), part_shape),
        in_specs=[vmem, vmem, vmem, smem, vmem, vmem, vmem],
        out_specs=(vmem, vmem, vmem),
        scratch_shapes=[pltpu.VMEM((4, 8, 128), f32), pltpu.VMEM((8, 128), jnp.int32), pltpu.VMEM((8, 256), jnp.int32)] + WORK,
        name="atoms",
    )(positions, charges, atom_types, atom_counts, type_sigma.reshape(1, -1), type_epsilon.reshape(1, -1), pair_list)
    even = lax.all_to_all(send, AXES, 0, 0, axis_index_groups=swap_groups(sizes, FIRST_PAIRS), tiled=True)
    send, part = pl.pallas_call(
        relay_kernel,
        out_shape=(pltpu.VMEM((8, 9, 8, 128), f32), part_shape),
        in_specs=[vmem, vmem, vmem],
        out_specs=(vmem, vmem),
        scratch_shapes=WORK,
        name="relay",
    )(keep(own), keep(even), keep(part))
    odd = lax.all_to_all(send, AXES, 0, 0, axis_index_groups=swap_groups(sizes, [1 - start for start in FIRST_PAIRS]), tiled=True)
    return pl.pallas_call(
        force_kernel,
        out_shape=jax.ShapeDtypeStruct((3, 2, 2, 2, 128), f32),
        in_specs=[vmem] * 4,
        out_specs=vmem,
        scratch_shapes=[pltpu.VMEM((8, 8, 128), f32)] + WORK,
        name="forces",
    )(keep(own), keep(even), keep(odd), keep(part))


def solution(mesh):
    placed = (
        P(None, "gx", "gy", "gz", None),
        P("gx", "gy", "gz", None),
        P("gx", "gy", "gz", None),
        P("gx", "gy", "gz"),
        P(),
        P(),
        P(None, "gx", "gy", "gz", None),
    )
    return jax.shard_map(
        per_device,
        mesh=mesh,
        in_specs=placed,
        out_specs=P(None, "gx", "gy", "gz", None),
        check_vma=False,
    )
```

```python
import math

import jax
import jax.numpy as jnp
from jax import lax
from jax.experimental import pallas as pl
from jax.experimental.pallas import tpu as pltpu
from jax.sharding import PartitionSpec as P

AXES = ("gx", "gy", "gz")
FIRST_PAIRS = (0, 0, 0)
CUT = 144.0
WIDTH = 44.0
UNIT = 1.0 / math.sqrt(WIDTH)
EDGE = 12.0 * UNIT
CHARGE_UNIT = WIDTH ** -0.25
DEPTH_UNIT = math.sqrt(24.0)
FORCE_UNIT = 2.0 / WIDTH * math.sqrt(WIDTH)
COUNT_LANE = 27
LEFT_LANE = 28
META_ROW = 6
RELATIONS = [(r // 4, r // 2 % 2, r % 2) for r in range(1, 8)]
MAX_CHUNKS = 32


def parities():
    return [lax.rem(lax.axis_index(name) + start, 2) for name, start in zip(AXES, FIRST_PAIRS)]


def early_stages():
    x, y, z = [lax.axis_index(name) for name in AXES]
    last = lax.axis_size("gy") - 1
    corner = jnp.maximum(x, jnp.maximum(y, z)) < 2
    beside = jnp.logical_and(x < 3, jnp.logical_or(y < 3, y == last))
    first = jnp.logical_and(corner, x + y + z > 0)
    return first, jnp.logical_and(jnp.logical_or(x == 0, beside), jnp.logical_not(corner))


def free_cells(relation, fixed, choices):
    spans = [[fixed[a]] if relation[a] else list(range(choices)) for a in range(3)]
    return [(x, y, z) for x in spans[0] for y in spans[1] for z in spans[2]]


def atoms_kernel(pos_ref, charge_ref, type_ref, count_ref, sigma_ref, eps_ref, pair_ref, own_ref, send_ref, part_ref, rows_ref, kinds_ref, codes_ref, *work):
    for i in range(2):
        for j in range(2):
            at = pl.ds(4 * i + 2 * j, 2)
            for comp in range(3):
                rows_ref[comp, at, :] = pos_ref[comp, i, j]
            rows_ref[3, at, :] = charge_ref[i, j]
            kinds_ref[at, :] = type_ref[i, j]
    codes_ref[...] = jnp.full(codes_ref.shape, -1, jnp.int32)
    slots = pair_ref.shape[-1]
    codes_ref[0:1, 0:slots] = pair_ref[0, 0, 0]
    codes_ref[1:2, 0:slots] = pair_ref[1, 0, 0]

    cell = lax.broadcasted_iota(jnp.int32, (8, 128), 0)
    lane = lax.broadcasted_iota(jnp.int32, (8, 128), 1)
    count = jnp.zeros((8, 128), jnp.int32)
    for c in range(8):
        count = jnp.where(cell == c, count_ref[c // 4, c // 2 % 2, c % 2], count)
    live = lane < count
    kinds = kinds_ref[...]
    sigma = jnp.broadcast_to(sigma_ref[...] * (0.5 * UNIT), (8, 128))
    depth = jnp.broadcast_to(jnp.sqrt(eps_ref[...]) * DEPTH_UNIT, (8, 128))
    sigma = jnp.take_along_axis(sigma, kinds, axis=1, mode="promise_in_bounds")
    depth = jnp.take_along_axis(depth, kinds, axis=1, mode="promise_in_bounds")

    cells = codes_ref[0:1, :]
    codes = codes_ref[1:2, :]
    width = codes_ref.shape[1]
    is_cell = lax.broadcasted_iota(jnp.int32, (8, width), 0) == cells
    is_code = lax.broadcasted_iota(jnp.int32, (128, width), 0) == codes
    listed = lax.dot_general(
        jnp.where(is_cell, 1.0, 0.0).astype(jnp.bfloat16),
        jnp.where(is_code, 1.0, 0.0).astype(jnp.bfloat16),
        (((1,), (1,)), ((), ())),
        preferred_element_type=jnp.float32,
    )
    atoms = count.astype(jnp.float32)
    meta = jnp.where(jnp.logical_or(lane == COUNT_LANE, lane == LEFT_LANE), atoms, listed * atoms)

    values = [rows_ref[0] * UNIT, rows_ref[1] * UNIT, rows_ref[2] * UNIT]
    values.append(jnp.where(live, rows_ref[3] * CHARGE_UNIT, 0.0))
    values.append(jnp.where(live, sigma, 0.5 * UNIT))
    values.append(jnp.where(live, depth, 0.0))
    values += [meta, jnp.zeros((8, 128), jnp.float32)]
    for r in range(8):
        own_ref[:, r, :] = values[r]

    odd = parities()
    toward = [1 - b for b in odd]
    for rel in RELATIONS:
        slot = sum(lax.bitwise_xor(odd[a], rel[a]) * (4, 2, 1)[a] for a in range(3))
        for n, (x, y, z) in enumerate(free_cells(rel, toward, 2)):
            send_ref[slot, n] = own_ref[4 * x + 2 * y + z]
    part_ref[...] = jnp.zeros(part_ref.shape, jnp.float32)

    @pl.when(early_stages()[0])
    def _():
        work[1][...] = jnp.zeros(work[1].shape, jnp.int32)
        place(work[0], work[1], odd, own_ref, None, None)
        cell_forces(part_ref, None, None, *work)


def relay_kernel(own_ref, got_ref, before_ref, send_ref, part_ref, *work):
    odd = parities()
    for rel in RELATIONS:
        slot = sum(lax.bitwise_xor(1 - odd[a], rel[a]) * (4, 2, 1)[a] for a in range(3))
        for n, at in enumerate(free_cells(rel, odd, 3)):
            far = [isinstance(p, int) and p == 2 for p in at]
            if not any(far):
                send_ref[slot, n] = own_ref[4 * at[0] + 2 * at[1] + at[2]]
                continue
            source = sum(lax.bitwise_xor(odd[a], int(far[a])) * (4, 2, 1)[a] for a in range(3))
            m = 0
            for a in range(3):
                if not far[a]:
                    m = m * 2 + at[a]
            send_ref[slot, n] = got_ref[source, m]
    part_ref[...] = before_ref[...]

    @pl.when(early_stages()[1])
    def _():
        work[1][...] = jnp.zeros(work[1].shape, jnp.int32)
        place(work[0], work[1], odd, own_ref, got_ref, None)
        cell_forces(part_ref, None, None, *work)


def place(ext_ref, meta_ref, odd, own_ref, even_ref, odd_ref, even_done=0):
    spot = [[1, 2, 3 - 3 * odd[a], 3 * odd[a]] for a in range(3)]
    lane = lax.broadcasted_iota(jnp.int32, (1, 128), 1)

    def put(at, tile, done):
        where = spot[0][at[0]] * 16 + spot[1][at[1]] * 4 + spot[2][at[2]]
        ext_ref[where] = tile
        meta = tile[META_ROW:META_ROW + 1, :].astype(jnp.int32)
        meta_ref[pl.ds(where, 1), :] = jnp.where(jnp.logical_and(lane != COUNT_LANE, done > 0), 0, meta)

    for c in range(8):
        put((c // 4, c // 2 % 2, c % 2), own_ref[c], 0)
    for rel in RELATIONS:
        if even_ref is not None:
            slot = sum(lax.bitwise_xor(odd[a], rel[a]) * (4, 2, 1)[a] for a in range(3))
            for n, at in enumerate(free_cells(rel, (2, 2, 2), 2)):
                put(at, even_ref[slot, n], even_done)
        if odd_ref is not None:
            slot = sum(lax.bitwise_xor(1 - odd[a], rel[a]) * (4, 2, 1)[a] for a in range(3))
            for n, at in enumerate(free_cells(rel, (3, 3, 3), 3)):
                put(at, odd_ref[slot, n], 0)


def pair_terms(home, other):
    dx = home[0] - other[0]
    dy = home[1] - other[1]
    dz = home[2] - other[2]
    dist = dx * dx + dy * dy + dz * dz
    size = home[4] + other[4]
    size = size * size
    root = lax.rsqrt(dist + size)
    inverse = root * root
    ratio = size * inverse
    cube = ratio * ratio * ratio
    coulomb = home[3] * other[3] * root
    attract = home[5] * other[5] * cube
    repel = attract * cube
    core = repel - attract
    energy = core + 6.0 * coulomb
    slope = core + repel + coulomb
    inner = jnp.clip(CUT / WIDTH - dist, 0.0, 1.0)
    scale = inner * ((1.0 - inner) * energy + (inner * (1.5 - inner)) * inverse * slope)
    return scale * dx, scale * dy, scale * dz


WORK = [
    pltpu.VMEM((64, 8, 128), jnp.float32),
    pltpu.VMEM((64, 128), jnp.int32),
    pltpu.SMEM((64, 128), jnp.int32),
    pltpu.VMEM((8, MAX_CHUNKS, 8, 128), jnp.float32),
    pltpu.SMEM((8,), jnp.int32),
    pltpu.VMEM((8, 6, 128, 128), jnp.float32),
    pltpu.VMEM((8, 3, 128, 128), jnp.float32),
    pltpu.SemaphoreType.DMA(()),
]


def spatial(c):
    return (1 + c // 4) * 16 + (1 + c // 2 % 2) * 4 + 1 + c % 2


def cell_forces(rows_ref, before_ref, own_done, ext_ref, meta_ref, info_ref, list_ref, pairs_ref, home_ref, sums_ref, sem):
    copy = pltpu.make_async_copy(meta_ref, info_ref, sem)
    copy.start()
    part = lax.broadcasted_iota(jnp.int32, (32, 768), 0)
    column = lax.broadcasted_iota(jnp.int32, (32, 768), 1)
    pick = jnp.logical_and(lax.bitwise_and(part, 7) == lax.shift_right_logical(column, 7), part < 24)
    pick = jnp.where(pick, 1.0, 0.0).astype(jnp.bfloat16)
    for c in range(8):
        rest = ext_ref[spatial(c)]
        pieces = []
        for _ in range(3):
            pieces.append(rest.astype(jnp.bfloat16).astype(jnp.float32))
            rest = rest - pieces[-1]
        pieces.append(jnp.zeros((8, 128), jnp.float32))
        cols = jnp.transpose(jnp.concatenate(pieces, 0)).astype(jnp.bfloat16)
        wide = lax.dot_general(cols, pick, (((1,), (0,)), ((), ())), preferred_element_type=jnp.float32)
        for r in range(6):
            home_ref[c, r] = wide[:, 128 * r:128 * (r + 1)]
    copy.wait()
    lane = lax.broadcasted_iota(jnp.int32, (8, 128), 1)
    row = lax.broadcasted_iota(jnp.int32, (8, 128), 0)
    filler = jnp.where(row < 3, 100.0, jnp.where(row == 4, 0.5 * UNIT, 0.0))

    def shift(move):
        vector = jnp.zeros((8, 128), jnp.float32)
        for a in range(3):
            if move[a]:
                vector = jnp.where(row == a, move[a] * EDGE, vector)
        return vector

    own_spots = [spatial(c) for c in range(8)]
    for c in range(8):
        here = spatial(c)
        end = jnp.int32(0)
        current = filler
        for code in range(27):
            move = (code // 9 - 1, code // 3 % 3 - 1, code % 3 - 1)
            there = here + move[0] * 16 + move[1] * 4 + move[2]
            size = jnp.where(info_ref[here, code] > 0, info_ref[there, LEFT_LANE], info_ref[there, 26 - code])
            if own_done is not None and there in own_spots:
                size = jnp.where(own_done, 0, size)
            chunk = lax.shift_right_logical(end, 7)
            first = lax.bitwise_and(end, 127)
            tile = pltpu.roll(ext_ref[there] + shift(move), first, axis=1)
            merged = jnp.where(lane < first, current, tile)
            list_ref[c, chunk] = merged
            end = end + size
            current = jnp.where(lax.shift_right_logical(end, 7) > chunk, tile, merged)
        chunk = lax.shift_right_logical(end, 7)
        list_ref[c, chunk] = jnp.where(lane < lax.bitwise_and(end, 127), current, filler)
        list_ref[c, chunk + 1] = filler
        pairs_ref[c] = lax.shift_right_logical(end + 255, 8)

    def cell_step(c, carry):
        here = (1 + c // 4) * 16 + (1 + c // 2 % 2) * 4 + 1 + c % 2
        atoms = info_ref[here, COUNT_LANE]
        pairs = pairs_ref[c]

        def group_step(g, carry):
            first = pl.multiple_of(g * 16, 16)
            homes = []
            for h in range(2):
                homes.append([home_ref[c, r, pl.ds(first + 8 * h, 8), :] for r in range(6)])

            def chunk_step(start, width, sums):
                sums = list(sums)
                for u in range(width):
                    other = [jnp.broadcast_to(list_ref[c, start + u, r:r + 1, :], (8, 128)) for r in range(6)]
                    for h in range(2):
                        terms = pair_terms(homes[h], other)
                        for a in range(3):
                            sums[3 * h + a] = sums[3 * h + a] + terms[a]
                return tuple(sums)

            fours = lax.shift_right_logical(pairs, 1)
            sums = (jnp.zeros((8, 128), jnp.float32),) * 6
            sums = lax.fori_loop(0, fours, lambda k, x: chunk_step(4 * k, 4, x), sums)
            sums = lax.fori_loop(2 * fours, pairs, lambda k, x: chunk_step(2 * k, 2, x), sums)
            for h in range(2):
                for a in range(3):
                    sums_ref[c, a, pl.ds(first + 8 * h, 8), :] = sums[3 * h + a]
            return carry

        lax.fori_loop(0, lax.shift_right_logical(atoms + 15, 4), group_step, 0)
        return carry

    lax.fori_loop(0, 8, cell_step, 0)
    comp = lax.broadcasted_iota(jnp.int32, (128, 8), 1)
    for c in range(8):
        total = [jnp.sum(sums_ref[c, a], axis=1, keepdims=True) for a in range(3)]
        line = jnp.where(comp == 0, total[0], jnp.where(comp == 1, total[1], total[2]))
        atoms = info_ref[spatial(c), COUNT_LANE]
        rows = jnp.where(lane < atoms, jnp.transpose(line), 0.0)
        rows_ref[c] = rows if before_ref is None else rows + before_ref[c]


def force_kernel(own_ref, even_ref, odd_ref, before_ref, out_ref, rows_ref, *work):
    first, second = early_stages()
    place(work[0], work[1], parities(), own_ref, even_ref, odd_ref, jnp.where(second, 1, 0))
    cell_forces(rows_ref, before_ref, jnp.logical_or(first, second), *work)
    for c in range(8):
        for a in range(3):
            out_ref[a, c // 4, c // 2 % 2, c % 2:c % 2 + 1, :] = rows_ref[c, a:a + 1, :] * FORCE_UNIT


def swap_groups(sizes, start):
    def index(x, y, z):
        return ((x % sizes[0]) * sizes[1] + y % sizes[1]) * sizes[2] + z % sizes[2]

    bits = [(b // 4, b // 2 % 2, b % 2) for b in range(8)]
    return [
        [index(x + start[0] + bx, y + start[1] + by, z + start[2] + bz) for bx, by, bz in bits]
        for x in range(0, sizes[0], 2)
        for y in range(0, sizes[1], 2)
        for z in range(0, sizes[2], 2)
    ]


def per_device(positions, charges, atom_types, atom_counts, type_sigma, type_epsilon, pair_list):
    f32 = jnp.float32
    sizes = [lax.axis_size(name) for name in AXES]
    vmem = pl.BlockSpec(memory_space=pltpu.VMEM)
    smem = pl.BlockSpec(memory_space=pltpu.SMEM)
    part_shape = pltpu.VMEM((8, 8, 128), f32)
    keep = lambda x: pltpu.with_memory_space_constraint(x, pltpu.VMEM)
    own, send, part = pl.pallas_call(
        atoms_kernel,
        out_shape=(part_shape, pltpu.VMEM((8, 4, 8, 128), f32), part_shape),
        in_specs=[vmem, vmem, vmem, smem, vmem, vmem, vmem],
        out_specs=(vmem, vmem, vmem),
        scratch_shapes=[pltpu.VMEM((4, 8, 128), f32), pltpu.VMEM((8, 128), jnp.int32), pltpu.VMEM((8, 256), jnp.int32)] + WORK,
        name="atoms",
    )(positions, charges, atom_types, atom_counts, type_sigma.reshape(1, -1), type_epsilon.reshape(1, -1), pair_list)
    even = lax.all_to_all(send, AXES, 0, 0, axis_index_groups=swap_groups(sizes, FIRST_PAIRS), tiled=True)
    send, part = pl.pallas_call(
        relay_kernel,
        out_shape=(pltpu.VMEM((8, 9, 8, 128), f32), part_shape),
        in_specs=[vmem, vmem, vmem],
        out_specs=(vmem, vmem),
        scratch_shapes=WORK,
        name="relay",
    )(keep(own), keep(even), keep(part))
    odd = lax.all_to_all(send, AXES, 0, 0, axis_index_groups=swap_groups(sizes, [1 - start for start in FIRST_PAIRS]), tiled=True)
    return pl.pallas_call(
        force_kernel,
        out_shape=jax.ShapeDtypeStruct((3, 2, 2, 2, 128), f32),
        in_specs=[vmem] * 4,
        out_specs=vmem,
        scratch_shapes=[pltpu.VMEM((8, 8, 128), f32)] + WORK,
        name="forces",
    )(keep(own), keep(even), keep(odd), keep(part))


def solution(mesh):
    placed = (
        P(None, "gx", "gy", "gz", None),
        P("gx", "gy", "gz", None),
        P("gx", "gy", "gz", None),
        P("gx", "gy", "gz"),
        P(),
        P(),
        P(None, "gx", "gy", "gz", None),
    )
    return jax.shard_map(
        per_device,
        mesh=mesh,
        in_specs=placed,
        out_specs=P(None, "gx", "gy", "gz", None),
        check_vma=False,
    )
```

```python
import math

import jax
import jax.numpy as jnp
from jax import lax
from jax.experimental import pallas as pl
from jax.experimental.pallas import tpu as pltpu
from jax.sharding import PartitionSpec as P

AXES = ("gx", "gy", "gz")
FIRST_PAIRS = (0, 0, 0)
CUT = 144.0
WIDTH = 44.0
UNIT = 1.0 / math.sqrt(WIDTH)
EDGE = 12.0 * UNIT
CHARGE_UNIT = WIDTH ** -0.25
DEPTH_UNIT = math.sqrt(24.0)
FORCE_UNIT = 2.0 / WIDTH * math.sqrt(WIDTH)
COUNT_LANE = 27
LEFT_LANE = 28
META_ROW = 6
RELATIONS = [(r // 4, r // 2 % 2, r % 2) for r in range(1, 8)]
MAX_CHUNKS = 32


def parities():
    return [lax.rem(lax.axis_index(name) + start, 2) for name, start in zip(AXES, FIRST_PAIRS)]


def early_stages():
    x, y, z = [lax.axis_index(name) for name in AXES]
    last = lax.axis_size("gy") - 1
    corner = jnp.maximum(x, jnp.maximum(y, z)) < 2
    beside = jnp.logical_and(x < 3, jnp.logical_or(y < 3, y == last))
    first = jnp.logical_and(corner, x + y + z > 0)
    return first, jnp.logical_and(jnp.logical_or(x == 0, beside), jnp.logical_not(corner))


def free_cells(relation, fixed, choices):
    spans = [[fixed[a]] if relation[a] else list(range(choices)) for a in range(3)]
    return [(x, y, z) for x in spans[0] for y in spans[1] for z in spans[2]]


def shipped(own_ref, cell):
    tile = own_ref[cell]
    return [(0, tile[0:4, :]), (4, tile[7:8, :])], tile[META_ROW:META_ROW + 1, :]


def pack(send_ref, slot, most, cells):
    lane = lax.broadcasted_iota(jnp.int32, (1, 128), 1)
    flags = None
    for n, (pieces, meta) in enumerate(cells):
        for row, piece in pieces:
            send_ref[slot, 5 * n + row:5 * n + row + piece.shape[0], :] = piece
        meta = jnp.where(lane < 32, meta, 0.0)
        flags = meta if n % 4 == 0 else flags + pltpu.roll(meta, 32 * (n % 4), axis=1)
        if n % 4 == 3 or n == len(cells) - 1:
            send_ref[slot, 5 * most + n // 4:5 * most + n // 4 + 1, :] = flags


def unpack(got_ref, slot, most, n):
    tile = got_ref[slot, 5 * n:5 * n + 8, :]
    meta = got_ref[slot, 5 * most + n // 4:5 * most + n // 4 + 1, :]
    if n % 4:
        meta = pltpu.roll(meta, 128 - 32 * (n % 4), axis=1)
    row = lax.broadcasted_iota(jnp.int32, (8, 128), 0)
    return jnp.where(row == 5, jnp.broadcast_to(meta, (8, 128)), tile)


def atoms_kernel(pos_ref, charge_ref, type_ref, count_ref, sigma_ref, eps_ref, pair_ref, own_ref, send_ref, part_ref, table_ref, rows_ref, kinds_ref, codes_ref, *work):
    for i in range(2):
        for j in range(2):
            at = pl.ds(4 * i + 2 * j, 2)
            for comp in range(3):
                rows_ref[comp, at, :] = pos_ref[comp, i, j]
            rows_ref[3, at, :] = charge_ref[i, j]
            kinds_ref[at, :] = type_ref[i, j]
    codes_ref[...] = jnp.full(codes_ref.shape, -1, jnp.int32)
    slots = pair_ref.shape[-1]
    codes_ref[0:1, 0:slots] = pair_ref[0, 0, 0]
    codes_ref[1:2, 0:slots] = pair_ref[1, 0, 0]

    cell = lax.broadcasted_iota(jnp.int32, (8, 128), 0)
    lane = lax.broadcasted_iota(jnp.int32, (8, 128), 1)
    count = jnp.zeros((8, 128), jnp.int32)
    for c in range(8):
        count = jnp.where(cell == c, count_ref[c // 4, c // 2 % 2, c % 2], count)
    live = lane < count
    kinds = kinds_ref[...]
    sigma = jnp.broadcast_to(sigma_ref[...] * (0.5 * UNIT), (8, 128))
    depth = jnp.broadcast_to(jnp.sqrt(eps_ref[...]) * DEPTH_UNIT, (8, 128))
    table_ref[...] = jnp.where(cell == 4, sigma, jnp.where(cell == 5, depth, 0.0))
    sigma = jnp.take_along_axis(sigma, kinds, axis=1, mode="promise_in_bounds")
    depth = jnp.take_along_axis(depth, kinds, axis=1, mode="promise_in_bounds")

    cells = codes_ref[0:1, :]
    codes = codes_ref[1:2, :]
    width = codes_ref.shape[1]
    is_cell = lax.broadcasted_iota(jnp.int32, (8, width), 0) == cells
    is_code = lax.broadcasted_iota(jnp.int32, (128, width), 0) == codes
    listed = lax.dot_general(
        jnp.where(is_cell, 1.0, 0.0).astype(jnp.bfloat16),
        jnp.where(is_code, 1.0, 0.0).astype(jnp.bfloat16),
        (((1,), (1,)), ((), ())),
        preferred_element_type=jnp.float32,
    )
    atoms = count.astype(jnp.float32)
    meta = jnp.where(jnp.logical_or(lane == COUNT_LANE, lane == LEFT_LANE), atoms, listed * atoms)

    values = [rows_ref[0] * UNIT, rows_ref[1] * UNIT, rows_ref[2] * UNIT]
    values.append(jnp.where(live, rows_ref[3] * CHARGE_UNIT, 0.0))
    values.append(jnp.where(live, sigma, 0.5 * UNIT))
    values.append(jnp.where(live, depth, 0.0))
    values += [meta, kinds.astype(jnp.float32)]
    for r in range(8):
        own_ref[:, r, :] = values[r]

    odd = parities()
    toward = [1 - b for b in odd]
    for rel in RELATIONS:
        slot = sum(lax.bitwise_xor(odd[a], rel[a]) * (4, 2, 1)[a] for a in range(3))
        pack(send_ref, slot, 4, [shipped(own_ref, 4 * x + 2 * y + z) for x, y, z in free_cells(rel, toward, 2)])
    part_ref[...] = jnp.zeros(part_ref.shape, jnp.float32)

    @pl.when(early_stages()[0])
    def _():
        work[1][...] = jnp.zeros(work[1].shape, jnp.int32)
        place(work[0], work[1], odd, table_ref, own_ref, None, None)
        cell_forces(part_ref, None, None, *work)


def relay_kernel(own_ref, got_ref, before_ref, table_ref, send_ref, part_ref, tiles_ref, *work):
    odd = parities()
    for rel in RELATIONS:
        slot = sum(lax.bitwise_xor(odd[a], rel[a]) * (4, 2, 1)[a] for a in range(3))
        for n in range(2 ** (3 - sum(rel))):
            tiles_ref[slot, n] = unpack(got_ref, slot, 4, n)
    for rel in RELATIONS:
        slot = sum(lax.bitwise_xor(1 - odd[a], rel[a]) * (4, 2, 1)[a] for a in range(3))
        cells = []
        for at in free_cells(rel, odd, 3):
            far = [isinstance(p, int) and p == 2 for p in at]
            if not any(far):
                cells.append(shipped(own_ref, 4 * at[0] + 2 * at[1] + at[2]))
                continue
            source = sum(lax.bitwise_xor(odd[a], int(far[a])) * (4, 2, 1)[a] for a in range(3))
            m = 0
            for a in range(3):
                if not far[a]:
                    m = m * 2 + at[a]
            tile = tiles_ref[source, m]
            cells.append(([(0, tile[0:5, :])], tile[5:6, :]))
        pack(send_ref, slot, 9, cells)
    part_ref[...] = before_ref[...]

    @pl.when(early_stages()[1])
    def _():
        work[1][...] = jnp.zeros(work[1].shape, jnp.int32)
        place(work[0], work[1], odd, table_ref, own_ref, got_ref, None)
        cell_forces(part_ref, None, None, *work)


def place(ext_ref, meta_ref, odd, table_ref, own_ref, even_ref, odd_ref, even_done=0):
    spot = [[1, 2, 3 - 3 * odd[a], 3 * odd[a]] for a in range(3)]
    lane = lax.broadcasted_iota(jnp.int32, (1, 128), 1)

    row = lax.broadcasted_iota(jnp.int32, (8, 128), 0)

    def arrived(got_ref, slot, most, n):
        tile = unpack(got_ref, slot, most, n)
        kinds = jnp.broadcast_to(tile[4:5, :], (8, 128)).astype(jnp.int32)
        kinds = jnp.clip(kinds, 0, 127)
        found = jnp.take_along_axis(table_ref[...], kinds, axis=1, mode="promise_in_bounds")
        return jnp.where(row < 4, tile, found), tile[5:6, :]

    def put(at, tile, meta, done):
        where = spot[0][at[0]] * 16 + spot[1][at[1]] * 4 + spot[2][at[2]]
        ext_ref[where] = tile
        meta = meta.astype(jnp.int32)
        meta_ref[pl.ds(where, 1), :] = jnp.where(jnp.logical_and(lane != COUNT_LANE, done > 0), 0, meta)

    for c in range(8):
        put((c // 4, c // 2 % 2, c % 2), own_ref[c], own_ref[c, META_ROW:META_ROW + 1, :], 0)
    for rel in RELATIONS:
        if even_ref is not None:
            slot = sum(lax.bitwise_xor(odd[a], rel[a]) * (4, 2, 1)[a] for a in range(3))
            for n, at in enumerate(free_cells(rel, (2, 2, 2), 2)):
                put(at, *arrived(even_ref, slot, 4, n), even_done)
        if odd_ref is not None:
            slot = sum(lax.bitwise_xor(1 - odd[a], rel[a]) * (4, 2, 1)[a] for a in range(3))
            for n, at in enumerate(free_cells(rel, (3, 3, 3), 3)):
                put(at, *arrived(odd_ref, slot, 9, n), 0)


def pair_terms(home, other):
    dx = home[0] - other[0]
    dy = home[1] - other[1]
    dz = home[2] - other[2]
    dist = dx * dx + dy * dy + dz * dz
    size = home[4] + other[4]
    size = size * size
    root = lax.rsqrt(dist + size)
    inverse = root * root
    ratio = size * inverse
    cube = ratio * ratio * ratio
    coulomb = home[3] * other[3] * root
    attract = home[5] * other[5] * cube
    repel = attract * cube
    core = repel - attract
    energy = core + 6.0 * coulomb
    slope = core + repel + coulomb
    inner = jnp.clip(CUT / WIDTH - dist, 0.0, 1.0)
    scale = inner * ((1.0 - inner) * energy + (inner * (1.5 - inner)) * inverse * slope)
    return scale * dx, scale * dy, scale * dz


WORK = [
    pltpu.VMEM((64, 8, 128), jnp.float32),
    pltpu.VMEM((64, 128), jnp.int32),
    pltpu.SMEM((64, 128), jnp.int32),
    pltpu.VMEM((8, MAX_CHUNKS, 8, 128), jnp.float32),
    pltpu.SMEM((8,), jnp.int32),
    pltpu.VMEM((8, 6, 128, 128), jnp.float32),
    pltpu.VMEM((8, 3, 128, 128), jnp.float32),
    pltpu.SemaphoreType.DMA(()),
]


def spatial(c):
    return (1 + c // 4) * 16 + (1 + c // 2 % 2) * 4 + 1 + c % 2


def cell_forces(rows_ref, before_ref, own_done, ext_ref, meta_ref, info_ref, list_ref, pairs_ref, home_ref, sums_ref, sem):
    copy = pltpu.make_async_copy(meta_ref, info_ref, sem)
    copy.start()
    part = lax.broadcasted_iota(jnp.int32, (32, 768), 0)
    column = lax.broadcasted_iota(jnp.int32, (32, 768), 1)
    pick = jnp.logical_and(lax.bitwise_and(part, 7) == lax.shift_right_logical(column, 7), part < 24)
    pick = jnp.where(pick, 1.0, 0.0).astype(jnp.bfloat16)
    for c in range(8):
        rest = ext_ref[spatial(c)]
        pieces = []
        for _ in range(3):
            pieces.append(rest.astype(jnp.bfloat16).astype(jnp.float32))
            rest = rest - pieces[-1]
        pieces.append(jnp.zeros((8, 128), jnp.float32))
        cols = jnp.transpose(jnp.concatenate(pieces, 0)).astype(jnp.bfloat16)
        wide = lax.dot_general(cols, pick, (((1,), (0,)), ((), ())), preferred_element_type=jnp.float32)
        for r in range(6):
            home_ref[c, r] = wide[:, 128 * r:128 * (r + 1)]
    copy.wait()
    lane = lax.broadcasted_iota(jnp.int32, (8, 128), 1)
    row = lax.broadcasted_iota(jnp.int32, (8, 128), 0)
    filler = jnp.where(row < 3, 100.0, jnp.where(row == 4, 0.5 * UNIT, 0.0))

    def shift(move):
        vector = jnp.zeros((8, 128), jnp.float32)
        for a in range(3):
            if move[a]:
                vector = jnp.where(row == a, move[a] * EDGE, vector)
        return vector

    own_spots = [spatial(c) for c in range(8)]
    for c in range(8):
        here = spatial(c)
        end = jnp.int32(0)
        current = filler
        for code in range(27):
            move = (code // 9 - 1, code // 3 % 3 - 1, code % 3 - 1)
            there = here + move[0] * 16 + move[1] * 4 + move[2]
            size = jnp.where(info_ref[here, code] > 0, info_ref[there, LEFT_LANE], info_ref[there, 26 - code])
            if own_done is not None and there in own_spots:
                size = jnp.where(own_done, 0, size)
            chunk = lax.shift_right_logical(end, 7)
            first = lax.bitwise_and(end, 127)
            tile = pltpu.roll(ext_ref[there] + shift(move), first, axis=1)
            merged = jnp.where(lane < first, current, tile)
            list_ref[c, chunk] = merged
            end = end + size
            current = jnp.where(lax.shift_right_logical(end, 7) > chunk, tile, merged)
        chunk = lax.shift_right_logical(end, 7)
        list_ref[c, chunk] = jnp.where(lane < lax.bitwise_and(end, 127), current, filler)
        list_ref[c, chunk + 1] = filler
        pairs_ref[c] = lax.shift_right_logical(end + 255, 8)

    def cell_step(c, carry):
        here = (1 + c // 4) * 16 + (1 + c // 2 % 2) * 4 + 1 + c % 2
        atoms = info_ref[here, COUNT_LANE]
        pairs = pairs_ref[c]

        def group_step(g, carry):
            first = pl.multiple_of(g * 16, 16)
            homes = []
            for h in range(2):
                homes.append([home_ref[c, r, pl.ds(first + 8 * h, 8), :] for r in range(6)])

            def chunk_step(start, width, sums):
                sums = list(sums)
                for u in range(width):
                    other = [jnp.broadcast_to(list_ref[c, start + u, r:r + 1, :], (8, 128)) for r in range(6)]
                    for h in range(2):
                        terms = pair_terms(homes[h], other)
                        for a in range(3):
                            sums[3 * h + a] = sums[3 * h + a] + terms[a]
                return tuple(sums)

            fours = lax.shift_right_logical(pairs, 1)
            sums = (jnp.zeros((8, 128), jnp.float32),) * 6
            sums = lax.fori_loop(0, fours, lambda k, x: chunk_step(4 * k, 4, x), sums)
            sums = lax.fori_loop(2 * fours, pairs, lambda k, x: chunk_step(2 * k, 2, x), sums)
            for h in range(2):
                for a in range(3):
                    sums_ref[c, a, pl.ds(first + 8 * h, 8), :] = sums[3 * h + a]
            return carry

        lax.fori_loop(0, lax.shift_right_logical(atoms + 15, 4), group_step, 0)
        return carry

    lax.fori_loop(0, 8, cell_step, 0)
    comp = lax.broadcasted_iota(jnp.int32, (128, 8), 1)
    for c in range(8):
        total = [jnp.sum(sums_ref[c, a], axis=1, keepdims=True) for a in range(3)]
        line = jnp.where(comp == 0, total[0], jnp.where(comp == 1, total[1], total[2]))
        atoms = info_ref[spatial(c), COUNT_LANE]
        rows = jnp.where(lane < atoms, jnp.transpose(line), 0.0)
        rows_ref[c] = rows if before_ref is None else rows + before_ref[c]


def force_kernel(own_ref, even_ref, odd_ref, before_ref, table_ref, out_ref, rows_ref, *work):
    first, second = early_stages()
    place(work[0], work[1], parities(), table_ref, own_ref, even_ref, odd_ref, jnp.where(second, 1, 0))
    cell_forces(rows_ref, before_ref, jnp.logical_or(first, second), *work)
    for c in range(8):
        for a in range(3):
            out_ref[a, c // 4, c // 2 % 2, c % 2:c % 2 + 1, :] = rows_ref[c, a:a + 1, :] * FORCE_UNIT


def swap_groups(sizes, start):
    def index(x, y, z):
        return ((x % sizes[0]) * sizes[1] + y % sizes[1]) * sizes[2] + z % sizes[2]

    bits = [(b // 4, b // 2 % 2, b % 2) for b in range(8)]
    return [
        [index(x + start[0] + bx, y + start[1] + by, z + start[2] + bz) for bx, by, bz in bits]
        for x in range(0, sizes[0], 2)
        for y in range(0, sizes[1], 2)
        for z in range(0, sizes[2], 2)
    ]


def per_device(positions, charges, atom_types, atom_counts, type_sigma, type_epsilon, pair_list):
    f32 = jnp.float32
    sizes = [lax.axis_size(name) for name in AXES]
    vmem = pl.BlockSpec(memory_space=pltpu.VMEM)
    smem = pl.BlockSpec(memory_space=pltpu.SMEM)
    part_shape = pltpu.VMEM((8, 8, 128), f32)
    keep = lambda x: pltpu.with_memory_space_constraint(x, pltpu.VMEM)
    own, send, part, table = pl.pallas_call(
        atoms_kernel,
        out_shape=(part_shape, pltpu.VMEM((8, 24, 128), f32), part_shape, pltpu.VMEM((8, 128), f32)),
        in_specs=[vmem, vmem, vmem, smem, vmem, vmem, vmem],
        out_specs=(vmem,) * 4,
        scratch_shapes=[pltpu.VMEM((4, 8, 128), f32), pltpu.VMEM((8, 128), jnp.int32), pltpu.VMEM((8, 256), jnp.int32)] + WORK,
        name="atoms",
    )(positions, charges, atom_types, atom_counts, type_sigma.reshape(1, -1), type_epsilon.reshape(1, -1), pair_list)
    even = lax.all_to_all(send, AXES, 0, 0, axis_index_groups=swap_groups(sizes, FIRST_PAIRS), tiled=True)
    send, part = pl.pallas_call(
        relay_kernel,
        out_shape=(pltpu.VMEM((8, 48, 128), f32), part_shape),
        in_specs=[vmem] * 4,
        out_specs=(vmem, vmem),
        scratch_shapes=[pltpu.VMEM((8, 4, 8, 128), f32)] + WORK,
        name="relay",
    )(keep(own), keep(even), keep(part), keep(table))
    odd = lax.all_to_all(send, AXES, 0, 0, axis_index_groups=swap_groups(sizes, [1 - start for start in FIRST_PAIRS]), tiled=True)
    return pl.pallas_call(
        force_kernel,
        out_shape=jax.ShapeDtypeStruct((3, 2, 2, 2, 128), f32),
        in_specs=[vmem] * 5,
        out_specs=vmem,
        scratch_shapes=[pltpu.VMEM((8, 8, 128), f32)] + WORK,
        name="forces",
    )(keep(own), keep(even), keep(odd), keep(part), keep(table))


def solution(mesh):
    placed = (
        P(None, "gx", "gy", "gz", None),
        P("gx", "gy", "gz", None),
        P("gx", "gy", "gz", None),
        P("gx", "gy", "gz"),
        P(),
        P(),
        P(None, "gx", "gy", "gz", None),
    )
    return jax.shard_map(
        per_device,
        mesh=mesh,
        in_specs=placed,
        out_specs=P(None, "gx", "gy", "gz", None),
        check_vma=False,
    )
```

```python
import math

import jax
import jax.numpy as jnp
from jax import lax
from jax.experimental import pallas as pl
from jax.experimental.pallas import tpu as pltpu
from jax.sharding import PartitionSpec as P

AXES = ("gx", "gy", "gz")
FIRST_PAIRS = (0, 0, 0)
CUT = 144.0
WIDTH = 44.0
UNIT = 1.0 / math.sqrt(WIDTH)
EDGE = 12.0 * UNIT
CHARGE_UNIT = WIDTH ** -0.25
DEPTH_UNIT = math.sqrt(24.0)
FORCE_UNIT = 2.0 / WIDTH * math.sqrt(WIDTH)
COUNT_LANE = 27
LEFT_LANE = 28
META_ROW = 6
RELATIONS = [(r // 4, r // 2 % 2, r % 2) for r in range(1, 8)]
MAX_CHUNKS = 32


def parities():
    return [lax.rem(lax.axis_index(name) + start, 2) for name, start in zip(AXES, FIRST_PAIRS)]


def early_stages():
    x, y, z = [lax.axis_index(name) for name in AXES]
    last = lax.axis_size("gy") - 1
    corner = jnp.maximum(x, jnp.maximum(y, z)) < 2
    beside = jnp.logical_and(x < 3, jnp.logical_or(y < 3, y == last))
    first = jnp.logical_and(corner, x + y + z > 0)
    return first, jnp.logical_and(jnp.logical_or(x == 0, beside), jnp.logical_not(corner))


def free_cells(relation, fixed, choices):
    spans = [[fixed[a]] if relation[a] else list(range(choices)) for a in range(3)]
    return [(x, y, z) for x in spans[0] for y in spans[1] for z in spans[2]]


def shipped(own_ref, cell):
    tile = own_ref[cell]
    return [(0, tile[0:4, :]), (4, tile[7:8, :])], tile[META_ROW:META_ROW + 1, :]


def pack(send_ref, slot, most, cells):
    lane = lax.broadcasted_iota(jnp.int32, (1, 128), 1)
    flags = None
    for n, (pieces, meta) in enumerate(cells):
        for row, piece in pieces:
            send_ref[slot, 5 * n + row:5 * n + row + piece.shape[0], :] = piece
        meta = jnp.where(lane < 32, meta, 0.0)
        flags = meta if n % 4 == 0 else flags + pltpu.roll(meta, 32 * (n % 4), axis=1)
        if n % 4 == 3 or n == len(cells) - 1:
            send_ref[slot, 5 * most + n // 4:5 * most + n // 4 + 1, :] = flags


def unpack(got_ref, slot, most, n):
    tile = got_ref[slot, 5 * n:5 * n + 8, :]
    meta = got_ref[slot, 5 * most + n // 4:5 * most + n // 4 + 1, :]
    if n % 4:
        meta = pltpu.roll(meta, 128 - 32 * (n % 4), axis=1)
    row = lax.broadcasted_iota(jnp.int32, (8, 128), 0)
    return jnp.where(row == 5, jnp.broadcast_to(meta, (8, 128)), tile)


def atoms_kernel(pos_ref, charge_ref, type_ref, count_ref, sigma_ref, eps_ref, pair_ref, own_ref, send_ref, part_ref, table_ref, rows_ref, kinds_ref, codes_ref, *work):
    for i in range(2):
        for j in range(2):
            at = pl.ds(4 * i + 2 * j, 2)
            for comp in range(3):
                rows_ref[comp, at, :] = pos_ref[comp, i, j]
            rows_ref[3, at, :] = charge_ref[i, j]
            kinds_ref[at, :] = type_ref[i, j]
    codes_ref[...] = jnp.full(codes_ref.shape, -1, jnp.int32)
    slots = pair_ref.shape[-1]
    codes_ref[0:1, 0:slots] = pair_ref[0, 0, 0]
    codes_ref[1:2, 0:slots] = pair_ref[1, 0, 0]

    cell = lax.broadcasted_iota(jnp.int32, (8, 128), 0)
    lane = lax.broadcasted_iota(jnp.int32, (8, 128), 1)
    count = jnp.zeros((8, 128), jnp.int32)
    for c in range(8):
        count = jnp.where(cell == c, count_ref[c // 4, c // 2 % 2, c % 2], count)
    live = lane < count
    kinds = kinds_ref[...]
    sigma = jnp.broadcast_to(sigma_ref[...] * (0.5 * UNIT), (8, 128))
    depth = jnp.broadcast_to(jnp.sqrt(eps_ref[...]) * DEPTH_UNIT, (8, 128))
    table_ref[...] = jnp.where(cell == 4, sigma, jnp.where(cell == 5, depth, 0.0))
    sigma = jnp.take_along_axis(sigma, kinds, axis=1, mode="promise_in_bounds")
    depth = jnp.take_along_axis(depth, kinds, axis=1, mode="promise_in_bounds")

    cells = codes_ref[0:1, :]
    codes = codes_ref[1:2, :]
    width = codes_ref.shape[1]
    is_cell = lax.broadcasted_iota(jnp.int32, (8, width), 0) == cells
    is_code = lax.broadcasted_iota(jnp.int32, (128, width), 0) == codes
    listed = lax.dot_general(
        jnp.where(is_cell, 1.0, 0.0).astype(jnp.bfloat16),
        jnp.where(is_code, 1.0, 0.0).astype(jnp.bfloat16),
        (((1,), (1,)), ((), ())),
        preferred_element_type=jnp.float32,
    )
    atoms = count.astype(jnp.float32)
    meta = jnp.where(jnp.logical_or(lane == COUNT_LANE, lane == LEFT_LANE), atoms, listed * atoms)

    values = [rows_ref[0] * UNIT, rows_ref[1] * UNIT, rows_ref[2] * UNIT]
    values.append(jnp.where(live, rows_ref[3] * CHARGE_UNIT, 0.0))
    values.append(jnp.where(live, sigma, 0.5 * UNIT))
    values.append(jnp.where(live, depth, 0.0))
    values += [meta, kinds.astype(jnp.float32)]
    for r in range(8):
        own_ref[:, r, :] = values[r]

    odd = parities()
    toward = [1 - b for b in odd]
    for rel in RELATIONS:
        slot = sum(lax.bitwise_xor(odd[a], rel[a]) * (4, 2, 1)[a] for a in range(3))
        pack(send_ref, slot, 4, [shipped(own_ref, 4 * x + 2 * y + z) for x, y, z in free_cells(rel, toward, 2)])
    part_ref[...] = jnp.zeros(part_ref.shape, jnp.float32)

    @pl.when(early_stages()[0])
    def _():
        work[1][...] = jnp.zeros(work[1].shape, jnp.int32)
        place(work[0], work[1], odd, table_ref, own_ref, None, None)
        cell_forces(part_ref, None, None, *work)


def relay_kernel(own_ref, got_ref, before_ref, table_ref, send_ref, part_ref, tiles_ref, *work):
    odd = parities()
    for rel in RELATIONS:
        slot = sum(lax.bitwise_xor(odd[a], rel[a]) * (4, 2, 1)[a] for a in range(3))
        for n in range(2 ** (3 - sum(rel))):
            tiles_ref[slot, n] = unpack(got_ref, slot, 4, n)
    for rel in RELATIONS:
        slot = sum(lax.bitwise_xor(1 - odd[a], rel[a]) * (4, 2, 1)[a] for a in range(3))
        cells = []
        for at in free_cells(rel, odd, 3):
            far = [isinstance(p, int) and p == 2 for p in at]
            if not any(far):
                cells.append(shipped(own_ref, 4 * at[0] + 2 * at[1] + at[2]))
                continue
            source = sum(lax.bitwise_xor(odd[a], int(far[a])) * (4, 2, 1)[a] for a in range(3))
            m = 0
            for a in range(3):
                if not far[a]:
                    m = m * 2 + at[a]
            tile = tiles_ref[source, m]
            cells.append(([(0, tile[0:5, :])], tile[5:6, :]))
        pack(send_ref, slot, 9, cells)
    part_ref[...] = before_ref[...]

    @pl.when(early_stages()[1])
    def _():
        work[1][...] = jnp.zeros(work[1].shape, jnp.int32)
        place(work[0], work[1], odd, table_ref, own_ref, got_ref, None)
        cell_forces(part_ref, None, None, *work)


def place(ext_ref, meta_ref, odd, table_ref, own_ref, even_ref, odd_ref, even_done=0):
    spot = [[1, 2, 3 - 3 * odd[a], 3 * odd[a]] for a in range(3)]
    lane = lax.broadcasted_iota(jnp.int32, (1, 128), 1)

    row = lax.broadcasted_iota(jnp.int32, (8, 128), 0)

    def arrived(got_ref, slot, most, n):
        tile = unpack(got_ref, slot, most, n)
        kinds = jnp.broadcast_to(tile[4:5, :], (8, 128)).astype(jnp.int32)
        kinds = jnp.clip(kinds, 0, 127)
        found = jnp.take_along_axis(table_ref[...], kinds, axis=1, mode="promise_in_bounds")
        return jnp.where(row < 4, tile, found), tile[5:6, :]

    def put(at, tile, meta, done):
        where = spot[0][at[0]] * 16 + spot[1][at[1]] * 4 + spot[2][at[2]]
        ext_ref[where] = tile
        meta = meta.astype(jnp.int32)
        meta_ref[pl.ds(where, 1), :] = jnp.where(jnp.logical_and(lane != COUNT_LANE, done > 0), 0, meta)

    for c in range(8):
        put((c // 4, c // 2 % 2, c % 2), own_ref[c], own_ref[c, META_ROW:META_ROW + 1, :], 0)
    for rel in RELATIONS:
        if even_ref is not None:
            slot = sum(lax.bitwise_xor(odd[a], rel[a]) * (4, 2, 1)[a] for a in range(3))
            for n, at in enumerate(free_cells(rel, (2, 2, 2), 2)):
                put(at, *arrived(even_ref, slot, 4, n), even_done)
        if odd_ref is not None:
            slot = sum(lax.bitwise_xor(1 - odd[a], rel[a]) * (4, 2, 1)[a] for a in range(3))
            for n, at in enumerate(free_cells(rel, (3, 3, 3), 3)):
                put(at, *arrived(odd_ref, slot, 9, n), 0)


def pair_terms(home, other):
    dx = home[0] - other[0]
    dy = home[1] - other[1]
    dz = home[2] - other[2]
    dist = dx * dx + dy * dy + dz * dz
    size = home[4] + other[4]
    size = size * size
    root = lax.rsqrt(dist + size)
    inverse = root * root
    ratio = size * inverse
    cube = ratio * ratio * ratio
    coulomb = home[3] * other[3] * root
    attract = home[5] * other[5] * cube
    repel = attract * cube
    core = repel - attract
    energy = core + 6.0 * coulomb
    slope = core + repel + coulomb
    inner = jnp.clip(CUT / WIDTH - dist, 0.0, 1.0)
    scale = inner * ((1.0 - inner) * energy + (inner * (1.5 - inner)) * inverse * slope)
    return scale * dx, scale * dy, scale * dz


WORK = [
    pltpu.VMEM((64, 8, 128), jnp.float32),
    pltpu.VMEM((64, 128), jnp.int32),
    pltpu.SMEM((64, 128), jnp.int32),
    pltpu.VMEM((8, MAX_CHUNKS, 8, 128), jnp.float32),
    pltpu.SMEM((8,), jnp.int32),
    pltpu.VMEM((8, 6, 128, 128), jnp.float32),
    pltpu.VMEM((8, 3, 128, 128), jnp.float32),
    pltpu.SemaphoreType.DMA(()),
]


def spatial(c):
    return (1 + c // 4) * 16 + (1 + c // 2 % 2) * 4 + 1 + c % 2


def cell_forces(rows_ref, before_ref, own_done, ext_ref, meta_ref, info_ref, list_ref, pairs_ref, home_ref, sums_ref, sem):
    copy = pltpu.make_async_copy(meta_ref, info_ref, sem)
    copy.start()
    part = lax.broadcasted_iota(jnp.int32, (32, 768), 0)
    column = lax.broadcasted_iota(jnp.int32, (32, 768), 1)
    pick = jnp.logical_and(lax.bitwise_and(part, 7) == lax.shift_right_logical(column, 7), part < 24)
    pick = jnp.where(pick, 1.0, 0.0).astype(jnp.bfloat16)
    for c in range(8):
        rest = ext_ref[spatial(c)]
        pieces = []
        for _ in range(3):
            pieces.append(rest.astype(jnp.bfloat16).astype(jnp.float32))
            rest = rest - pieces[-1]
        pieces.append(jnp.zeros((8, 128), jnp.float32))
        cols = jnp.transpose(jnp.concatenate(pieces, 0)).astype(jnp.bfloat16)
        wide = lax.dot_general(cols, pick, (((1,), (0,)), ((), ())), preferred_element_type=jnp.float32)
        for r in range(6):
            home_ref[c, r] = wide[:, 128 * r:128 * (r + 1)]
    copy.wait()
    lane = lax.broadcasted_iota(jnp.int32, (8, 128), 1)
    row = lax.broadcasted_iota(jnp.int32, (8, 128), 0)
    filler = jnp.where(row < 3, 100.0, jnp.where(row == 4, 0.5 * UNIT, 0.0))

    def shift(move):
        vector = jnp.zeros((8, 128), jnp.float32)
        for a in range(3):
            if move[a]:
                vector = jnp.where(row == a, move[a] * EDGE, vector)
        return vector

    own_spots = [spatial(c) for c in range(8)]
    for c in range(8):
        here = spatial(c)
        end = jnp.int32(0)
        current = filler
        for code in range(27):
            move = (code // 9 - 1, code // 3 % 3 - 1, code % 3 - 1)
            there = here + move[0] * 16 + move[1] * 4 + move[2]
            size = jnp.where(info_ref[here, code] > 0, info_ref[there, LEFT_LANE], info_ref[there, 26 - code])
            if own_done is not None and there in own_spots:
                size = jnp.where(own_done, 0, size)
            chunk = lax.shift_right_logical(end, 7)
            first = lax.bitwise_and(end, 127)
            tile = pltpu.roll(ext_ref[there] + shift(move), first, axis=1)
            merged = jnp.where(lane < first, current, tile)
            list_ref[c, chunk] = merged
            end = end + size
            current = jnp.where(lax.shift_right_logical(end, 7) > chunk, tile, merged)
        chunk = lax.shift_right_logical(end, 7)
        list_ref[c, chunk] = jnp.where(lane < lax.bitwise_and(end, 127), current, filler)
        list_ref[c, chunk + 1] = filler
        pairs_ref[c] = lax.shift_right_logical(end + 255, 8)

    def cell_step(c, carry):
        here = (1 + c // 4) * 16 + (1 + c // 2 % 2) * 4 + 1 + c % 2
        atoms = info_ref[here, COUNT_LANE]
        pairs = pairs_ref[c]

        def group(first, tiles):
            homes = [[home_ref[c, r, pl.ds(first + 8 * h, 8), :] for r in range(6)] for h in range(tiles)]

            def chunk_step(start, width, sums):
                sums = list(sums)
                for u in range(width):
                    other = [jnp.broadcast_to(list_ref[c, start + u, r:r + 1, :], (8, 128)) for r in range(6)]
                    for h in range(tiles):
                        terms = pair_terms(homes[h], other)
                        for a in range(3):
                            sums[3 * h + a] = sums[3 * h + a] + terms[a]
                return tuple(sums)

            fours = lax.shift_right_logical(pairs, 1)
            sums = (jnp.zeros((8, 128), jnp.float32),) * (3 * tiles)
            sums = lax.fori_loop(0, fours, lambda k, x: chunk_step(4 * k, 4, x), sums)
            sums = lax.fori_loop(2 * fours, pairs, lambda k, x: chunk_step(2 * k, 2, x), sums)
            for h in range(tiles):
                for a in range(3):
                    sums_ref[c, a, pl.ds(first + 8 * h, 8), :] = sums[3 * h + a]

        def group_step(g, carry):
            group(pl.multiple_of(g * 16, 16), 2)
            return carry

        eights = lax.shift_right_logical(atoms + 7, 3)
        lax.fori_loop(0, lax.shift_right_logical(eights, 1), group_step, 0)

        @pl.when(lax.bitwise_and(eights, 1) == 1)
        def _():
            group(pl.multiple_of((eights - 1) * 8, 8), 1)

        return carry

    lax.fori_loop(0, 8, cell_step, 0)
    comp = lax.broadcasted_iota(jnp.int32, (128, 8), 1)
    for c in range(8):
        total = [jnp.sum(sums_ref[c, a], axis=1, keepdims=True) for a in range(3)]
        line = jnp.where(comp == 0, total[0], jnp.where(comp == 1, total[1], total[2]))
        atoms = info_ref[spatial(c), COUNT_LANE]
        rows = jnp.where(lane < atoms, jnp.transpose(line), 0.0)
        rows_ref[c] = rows if before_ref is None else rows + before_ref[c]


def force_kernel(own_ref, even_ref, odd_ref, before_ref, table_ref, out_ref, rows_ref, *work):
    first, second = early_stages()
    place(work[0], work[1], parities(), table_ref, own_ref, even_ref, odd_ref, jnp.where(second, 1, 0))
    cell_forces(rows_ref, before_ref, jnp.logical_or(first, second), *work)
    for c in range(8):
        for a in range(3):
            out_ref[a, c // 4, c // 2 % 2, c % 2:c % 2 + 1, :] = rows_ref[c, a:a + 1, :] * FORCE_UNIT


def swap_groups(sizes, start):
    def index(x, y, z):
        return ((x % sizes[0]) * sizes[1] + y % sizes[1]) * sizes[2] + z % sizes[2]

    bits = [(b // 4, b // 2 % 2, b % 2) for b in range(8)]
    return [
        [index(x + start[0] + bx, y + start[1] + by, z + start[2] + bz) for bx, by, bz in bits]
        for x in range(0, sizes[0], 2)
        for y in range(0, sizes[1], 2)
        for z in range(0, sizes[2], 2)
    ]


def per_device(positions, charges, atom_types, atom_counts, type_sigma, type_epsilon, pair_list):
    f32 = jnp.float32
    sizes = [lax.axis_size(name) for name in AXES]
    vmem = pl.BlockSpec(memory_space=pltpu.VMEM)
    smem = pl.BlockSpec(memory_space=pltpu.SMEM)
    part_shape = pltpu.VMEM((8, 8, 128), f32)
    keep = lambda x: pltpu.with_memory_space_constraint(x, pltpu.VMEM)
    own, send, part, table = pl.pallas_call(
        atoms_kernel,
        out_shape=(part_shape, pltpu.VMEM((8, 24, 128), f32), part_shape, pltpu.VMEM((8, 128), f32)),
        in_specs=[vmem, vmem, vmem, smem, vmem, vmem, vmem],
        out_specs=(vmem,) * 4,
        scratch_shapes=[pltpu.VMEM((4, 8, 128), f32), pltpu.VMEM((8, 128), jnp.int32), pltpu.VMEM((8, 256), jnp.int32)] + WORK,
        name="atoms",
        compiler_params=pltpu.CompilerParams(),
    )(positions, charges, atom_types, atom_counts, type_sigma.reshape(1, -1), type_epsilon.reshape(1, -1), pair_list)
    even = lax.all_to_all(send, AXES, 0, 0, axis_index_groups=swap_groups(sizes, FIRST_PAIRS), tiled=True)
    send, part = pl.pallas_call(
        relay_kernel,
        out_shape=(pltpu.VMEM((8, 48, 128), f32), part_shape),
        in_specs=[vmem] * 4,
        out_specs=(vmem, vmem),
        scratch_shapes=[pltpu.VMEM((8, 4, 8, 128), f32)] + WORK,
        name="relay",
        compiler_params=pltpu.CompilerParams(),
    )(keep(own), keep(even), keep(part), keep(table))
    odd = lax.all_to_all(send, AXES, 0, 0, axis_index_groups=swap_groups(sizes, [1 - start for start in FIRST_PAIRS]), tiled=True)
    return pl.pallas_call(
        force_kernel,
        out_shape=jax.ShapeDtypeStruct((3, 2, 2, 2, 128), f32),
        in_specs=[vmem] * 5,
        out_specs=vmem,
        scratch_shapes=[pltpu.VMEM((8, 8, 128), f32)] + WORK,
        name="forces",
        compiler_params=pltpu.CompilerParams(),
    )(keep(own), keep(even), keep(odd), keep(part), keep(table))


def solution(mesh):
    placed = (
        P(None, "gx", "gy", "gz", None),
        P("gx", "gy", "gz", None),
        P("gx", "gy", "gz", None),
        P("gx", "gy", "gz"),
        P(),
        P(),
        P(None, "gx", "gy", "gz", None),
    )
    return jax.shard_map(
        per_device,
        mesh=mesh,
        in_specs=placed,
        out_specs=P(None, "gx", "gy", "gz", None),
        check_vma=False,
    )
```
